256 devices in a mesh: dp: 8 (over z_lo, core), mp: 16 (over x, y), group: 2 (over z_hi).
Axes of the slice: x: 4, y: 4, z: 8 (z_hi: 2, z_lo: 4; z = z_hi * 4 + z_lo), core: 2. Of those that a mesh axis runs over, the one named last changes fastest.
Arguments:
- hidden: bfloat16 [1024, 8192], P('dp', 'mp'), may hold values from -6 to 6
- neighbour_ids: int32 [16, 2, 128], P('dp', 'group'), may hold values from 0 to 65535, as said below
- counts: int32 [16], P('dp'), may hold values from 0 to 2
- embed_table: bfloat16 [65536, 8192], P(('dp', 'group'), 'mp'), may hold values from -6 to 6
- w_query: bfloat16 [8192, 4096], P('group', 'mp'), may hold values from -0.0625 to 0.0625
- w_key: bfloat16 [8192, 4096], P('group', 'mp'), may hold values from -0.0625 to 0.0625
- w_value: bfloat16 [8192, 4096], P('group', 'mp'), may hold values from -0.0625 to 0.0625
- w_out: bfloat16 [4096, 8192], P('mp', 'group'), may hold values from -0.09375 to 0.09375
- grad_out: bfloat16 [1024, 8192], P('dp', 'mp'), may hold values from -6 to 6
Outputs:
- output: float32 [1024, 8192], P('dp', 'mp')
- grad_hidden: float32 [1024, 8192], P('dp', 'mp')
- grad_neighbours: float32 [16, 2, 128, 8192], P('dp', 'group', None, 'mp')
The draws below stay inside these ranges and needn't reach their ends.
Inputs may be any that keep to these rules, and one draw needn't show every extreme that they name: `neighbour_ids`: token ids of the retrieved neighbours; the ids are split into 16 owners of 4096 consecutive ids each; of the 256 ids of one window's neighbour k (blocks of one window, one k), at most 64 belong to one owner, and exactly 64 belong to some owner. neighbours k < counts[c] of block c are used, the others are masked.
All inputs are finite; a program needn't handle non-finite values.
Results may differ from the reference program's by a relative error of at most 0.019.
Values may be sent and summed in bfloat16 or wider, within the bound.
A program may use at most 128 MiB of HBM per device.

```python
import math
import jax
import jax.numpy as jnp
from jax import lax

D = 8192
HEADS = 32
HD = 128
BLOCK = 64
RET = 128
NEIGH = 2
VOCAB = 65536
TOK_DEV = 128
HM = 2
BLK_DEV = 2
SEQS = 8
TOKENS = 1024
BLOCKS = 16
CAP = 64
N_DP = 8
N_MP = 16
N_GROUP = 2


def draw_neighbour_ids(key, part):
    owners = N_DP * N_GROUP
    slots = BLK_DEV * RET
    rows_per = VOCAB // owners
    key_perm = jax.random.fold_in(key, 11)
    key_order = jax.random.fold_in(key, 12)
    key_offset = jax.random.fold_in(key, 13)
    key_row_a = jax.random.fold_in(key, 14)
    key_row_b = jax.random.fold_in(key, 15)
    owner_perm = jax.vmap(lambda k: jax.random.permutation(k, owners))(jax.random.split(key_perm, owners))
    slot_order = jax.vmap(lambda k: jax.random.permutation(k, slots))(jax.random.split(key_order, owners))
    offsets = jax.random.randint(key_offset, (owners, 1), 0, owners - 1)
    slot_index = jnp.arange(slots, dtype=jnp.int32)[None, :]
    later = 1 + (slot_index - CAP + offsets) % (owners - 1)
    rank = jnp.where(slot_index < CAP, 0, later).astype(jnp.int32)
    owner_drawn = jnp.take_along_axis(owner_perm.astype(jnp.int32), rank, 1)
    owner_mixed = jnp.take_along_axis(owner_drawn, slot_order.astype(jnp.int32), 1)
    row_a = jax.random.randint(key_row_a, (owners, slots), 0, rows_per)
    row_b = jax.random.randint(key_row_b, (owners, slots), 0, rows_per)
    ids = owner_mixed * rows_per + jnp.minimum(row_a, row_b)
    ids = ids.reshape(N_DP, N_GROUP, BLK_DEV, RET)
    ids = jnp.transpose(ids, (0, 2, 1, 3)).reshape(BLOCKS, NEIGH, RET)
    return ids.astype(jnp.int32)


def set_ends(drawn, rng, low, largest):
    spot = [jax.random.randint(jax.random.fold_in(rng, axis), (), 0, length) for axis, length in enumerate(drawn.shape)]
    longest = drawn.shape.index(max(drawn.shape))
    next_to = spot[:longest] + [(spot[longest] + 1) % drawn.shape[longest]] + spot[longest + 1:]
    return drawn.at[tuple(spot)].set(low).at[tuple(next_to)].set(largest)


def block_levels(rng, shape, cuts, smallest, top_value):
    gain, own = 1.0, jax.random.fold_in(rng, 6)
    for position, parts in cuts:
        heights = jnp.exp(jax.random.uniform(jax.random.fold_in(own, position), (parts,), jnp.float32, smallest / len(cuts), top_value / len(cuts)))
        gain = gain * jnp.repeat(heights, shape[position] // parts).reshape([-1 if axis == position else 1 for axis in range(len(shape))])
    return gain


def centred(stream_key, dims, scale, limit, cuts=(), kind=jnp.bfloat16):
    array = jax.random.normal(stream_key, dims, jnp.float32) * scale
    if len(cuts) > 0:
        array = block_levels(stream_key, dims, cuts, -0.22, 0.18) * array
    return jnp.clip(array, min=-limit, max=limit).astype(kind)


def setup_inputs(seed: int = 0) -> dict:
    key_of = jax.random.split(jax.random.key(seed), 10)
    return {
        "hidden": centred(key_of[0], (TOKENS, D), 1.0, 6.0, ((0, 8), (1, 16))),
        "neighbour_ids": draw_neighbour_ids(jax.random.fold_in(key_of[9], 71), 0),
        "counts": set_ends(jax.random.randint(key_of[2], (BLOCKS,), 0, NEIGH + 1), jax.random.fold_in(key_of[2], 1), 0, NEIGH).astype(jnp.int32),
        "embed_table": centred(key_of[3], (VOCAB, D), 1.0, 6.0, ((0, 16), (1, 16))),
        "w_query": centred(key_of[4], (D, HEADS * HD), D ** -0.5, 0.0625, ((0, 2), (1, 16))),
        "w_key": centred(key_of[5], (D, HEADS * HD), D ** -0.5, 0.0625, ((0, 2), (1, 16))),
        "w_value": centred(key_of[6], (D, HEADS * HD), D ** -0.5, 0.0625, ((0, 2), (1, 16))),
        "w_out": centred(key_of[7], (HEADS * HD, D), (HEADS * HD) ** -0.5, 0.09375, ((0, 16), (1, 2))),
        "grad_out": centred(key_of[8], (TOKENS, D), 1.0, 6.0, ((0, 8), (1, 16))),
    }


def rounded(value):
    return lax.optimization_barrier(value.astype(jnp.bfloat16)).astype(jnp.float32)

def contract(left, right):
    return lax.dot_general(left, right, (((1,), (1,)), ((), ())), preferred_element_type=jnp.float32)

def window_ahead(rows, tail_rows):
    shaped = rows.reshape(SEQS, TOK_DEV, rows.shape[1])
    padding = jnp.zeros((SEQS, tail_rows, rows.shape[1]), rows.dtype)
    return jnp.concatenate([shaped[:, tail_rows:], padding], 1).reshape(TOKENS, rows.shape[1])

def window_back(rows, tail_rows):
    shaped = rows.reshape(SEQS, TOK_DEV, rows.shape[1])
    padding = jnp.zeros((SEQS, tail_rows, rows.shape[1]), rows.dtype)
    return jnp.concatenate([padding, shaped[:, :TOK_DEV - tail_rows]], 1).reshape(TOKENS, rows.shape[1])

def reference(hidden, neighbour_ids, counts, embed_table, w_query, w_key, w_value, w_out, grad_out):
    inv_root = 1.0 / math.sqrt(HD)
    tail_rows = BLOCK - 1
    width = HEADS * HD
    group_cols = HM * HD
    neighbours = embed_table[neighbour_ids.reshape(-1)]
    keys = jnp.dot(neighbours, w_key, preferred_element_type=jnp.float32).astype(jnp.bfloat16)
    values = jnp.dot(neighbours, w_value, preferred_element_type=jnp.float32).astype(jnp.bfloat16)
    key_block = keys.reshape(BLOCKS, NEIGH * RET, HEADS, HD).astype(jnp.float32)
    value_block = values.reshape(BLOCKS, NEIGH * RET, HEADS, HD).astype(jnp.float32)
    query_rows = window_ahead(hidden, tail_rows)
    query = jnp.dot(query_rows, w_query, preferred_element_type=jnp.float32).astype(jnp.bfloat16)
    query_block = query.reshape(BLOCKS, BLOCK, HEADS, HD).astype(jnp.float32)
    slot_of = jnp.arange(NEIGH * RET, dtype=jnp.int32) // RET
    live = (slot_of[None, :] < counts[:, None]).astype(jnp.float32)
    scores = jnp.einsum('cqhd,ckhd->chqk', query_block, key_block) * inv_root
    weights = jnp.exp(scores) * live[:, None, None, :]
    total = 1.0 + lax.optimization_barrier(jnp.sum(weights, -1))
    numer = jnp.einsum('chqk,ckhd->cqhd', rounded(weights), value_block)
    attn = numer / jnp.transpose(total, (0, 2, 1))[..., None]
    attn_bf = attn.reshape(TOKENS, width).astype(jnp.bfloat16)
    out_rows = jnp.zeros((TOKENS, D), jnp.float32)
    for group_index in range(N_MP):
        lo_col = group_index * group_cols
        part = jnp.dot(attn_bf[:, lo_col:lo_col + group_cols], w_out[lo_col:lo_col + group_cols], preferred_element_type=jnp.float32)
        out_rows = out_rows + rounded(part)
    output = window_back(out_rows, tail_rows)
    grad_rows = window_ahead(grad_out, tail_rows)
    d_attn = contract(grad_rows, w_out).astype(jnp.bfloat16)
    d_block = d_attn.reshape(BLOCKS, BLOCK, HEADS, HD).astype(jnp.float32)
    prob = weights / total[..., None]
    d_prob = jnp.einsum('cqhd,ckhd->chqk', d_block, value_block)
    delta = lax.optimization_barrier(jnp.sum(d_block * attn, -1))
    d_score = rounded(prob * (d_prob - jnp.transpose(delta, (0, 2, 1))[..., None]))
    d_query = (jnp.einsum('chqk,ckhd->cqhd', d_score, key_block) * inv_root).astype(jnp.bfloat16).reshape(TOKENS, width)
    d_keys = (jnp.einsum('chqk,cqhd->ckhd', d_score, query_block) * inv_root).astype(jnp.bfloat16).reshape(BLOCKS * NEIGH * RET, width)
    d_values = jnp.einsum('chqk,cqhd->ckhd', rounded(prob), d_block).astype(jnp.bfloat16).reshape(BLOCKS * NEIGH * RET, width)
    hid_rows = jnp.zeros((TOKENS, D), jnp.float32)
    neigh_rows = jnp.zeros((BLOCKS * NEIGH * RET, D), jnp.float32)
    for group_index in range(N_MP):
        lo_col = group_index * group_cols
        hi_col = lo_col + group_cols
        hid_rows = hid_rows + rounded(contract(d_query[:, lo_col:hi_col], w_query[:, lo_col:hi_col]))
        neigh_part = contract(d_keys[:, lo_col:hi_col], w_key[:, lo_col:hi_col]) + contract(d_values[:, lo_col:hi_col], w_value[:, lo_col:hi_col])
        neigh_rows = neigh_rows + rounded(neigh_part)
    grad_hidden = window_back(hid_rows, tail_rows)
    grad_neighbours = neigh_rows.reshape(BLOCKS, NEIGH, RET, D)
    return (output, grad_hidden, grad_neighbours)
```

```python
import math

import jax
import jax.numpy as jnp
from jax import lax
from jax.sharding import PartitionSpec as P

HD = 128
BLOCK = 64
RET = 128


def contract(left, right):
    return lax.dot_general(
        left, right, (((1,), (1,)), ((), ())), preferred_element_type=jnp.float32
    )


def per_device(
    hidden, neighbour_ids, counts, embed_table, w_query, w_key, w_value, w_out, grad_out
):
    tail_rows = BLOCK - 1
    rows_here = hidden.shape[0]
    blocks_here = rows_here // BLOCK
    heads_here = w_query.shape[1] // HD
    inv_root = 1.0 / math.sqrt(HD)
    keep_rows = rows_here - tail_rows
    pad_rows = jnp.zeros((tail_rows, hidden.shape[1]), jnp.bfloat16)
    query_rows = jnp.concatenate([hidden[tail_rows:], pad_rows], 0)
    grad_rows = jnp.concatenate([grad_out[tail_rows:], pad_rows], 0)
    full_query, full_grad = (
        lax.all_gather(query_rows, "mp", axis=1, tiled=True),
        lax.all_gather(grad_rows, "mp", axis=1, tiled=True),
    )
    flat_ids = neighbour_ids.reshape(-1)
    block_rows = embed_table.shape[0]
    owners = lax.axis_size("dp") * lax.axis_size("group")
    cap = flat_ids.shape[0] // 4
    every_id = lax.all_gather(
        flat_ids.astype(jnp.float32), ("dp", "group"), axis=0, tiled=True
    ).astype(jnp.int32).reshape(owners, -1)
    owner = lax.axis_index("dp") * lax.axis_size("group") + lax.axis_index("group")
    local_ids = every_id - owner * block_rows
    inside = (local_ids >= 0) & (local_ids < block_rows)
    rank = jnp.cumsum(inside.astype(jnp.int32), axis=1) - 1
    slot_hit = inside[:, :, None] & (rank[:, :, None] == jnp.arange(cap)[None, None, :])
    send_rows = jnp.sum(jnp.where(slot_hit, local_ids[:, :, None], 0), axis=1)
    send_buf = embed_table[send_rows.reshape(-1)].reshape(owners, cap, -1)
    recv_buf = lax.all_to_all(send_buf, ("dp", "group"), 0, 0, tiled=True)
    own_owner = flat_ids // block_rows
    same_owner = own_owner[:, None] == jnp.arange(owners)[None, :]
    own_rank = jnp.sum(
        jnp.where(same_owner, jnp.cumsum(same_owner.astype(jnp.int32), axis=0), 0), axis=1
    ) - 1
    own_cols = recv_buf.reshape(owners * cap, -1)[own_owner * cap + own_rank]
    neighbours = lax.all_gather(own_cols, "mp", axis=1, tiled=True)
    wq_full, wk_full, wv_full = (
        lax.all_gather(w_query, "group", axis=0, tiled=True),
        lax.all_gather(w_key, "group", axis=0, tiled=True),
        lax.all_gather(w_value, "group", axis=0, tiled=True),
    )
    query_sum = jnp.dot(full_query, wq_full, preferred_element_type=jnp.float32)
    query = query_sum.astype(jnp.bfloat16)
    wo_full = lax.all_gather(w_out, "group", axis=1, tiled=True)
    keys = jnp.dot(neighbours, wk_full, preferred_element_type=jnp.float32).astype(jnp.bfloat16)
    values = jnp.dot(neighbours, wv_full, preferred_element_type=jnp.float32).astype(jnp.bfloat16)
    key_block = keys.reshape(blocks_here, RET, heads_here, HD)
    value_block = values.reshape(blocks_here, RET, heads_here, HD)
    query_block = query.reshape(blocks_here, BLOCK, heads_here, HD)
    live = (counts > lax.axis_index("group")).astype(jnp.float32)
    scores = (
        jnp.einsum("cqhd,ckhd->chqk", query_block, key_block, preferred_element_type=jnp.float32)
        * inv_root
    )
    weights = jnp.exp(scores) * live[:, None, None, None]
    numer = jnp.einsum(
        "chqk,ckhd->cqhd",
        weights.astype(jnp.bfloat16),
        value_block,
        preferred_element_type=jnp.float32,
    )
    partial_total = jnp.sum(weights, -1)
    numer, partial_total = lax.psum((numer, partial_total), "group")
    total = partial_total + 1.0
    attn = numer / jnp.transpose(total, (0, 2, 1))[..., None]
    attn_bf = attn.reshape(rows_here, heads_here * HD).astype(jnp.bfloat16)
    out_term = jnp.dot(attn_bf, wo_full, preferred_element_type=jnp.float32)
    d_attn = contract(full_grad, wo_full).astype(jnp.bfloat16)
    d_block = d_attn.reshape(blocks_here, BLOCK, heads_here, HD)
    prob = weights / total[..., None]
    d_prob = jnp.einsum("cqhd,ckhd->chqk", d_block, value_block, preferred_element_type=jnp.float32)
    delta = jnp.sum(d_block.astype(jnp.float32) * attn, -1)
    d_score = (prob * (d_prob - jnp.transpose(delta, (0, 2, 1))[..., None])).astype(jnp.bfloat16)
    query_part = jnp.einsum(
        "chqk,ckhd->cqhd", d_score, key_block, preferred_element_type=jnp.float32
    )
    query_grad = lax.psum(query_part, "group")
    d_query = (query_grad * inv_root).astype(jnp.bfloat16).reshape(rows_here, heads_here * HD)
    d_keys = (
        jnp.einsum("chqk,cqhd->ckhd", d_score, query_block, preferred_element_type=jnp.float32)
        * inv_root
    ).astype(jnp.bfloat16)
    d_values = jnp.einsum(
        "chqk,cqhd->ckhd", prob.astype(jnp.bfloat16), d_block, preferred_element_type=jnp.float32
    ).astype(jnp.bfloat16)
    d_keys = d_keys.reshape(blocks_here * RET, heads_here * HD)
    d_values = d_values.reshape(blocks_here * RET, heads_here * HD)
    hid_term = contract(d_query, wq_full)
    out_cols, hid_cols = (
        lax.psum_scatter(
            out_term.astype(jnp.bfloat16), "mp", scatter_dimension=1, tiled=True
        ).astype(jnp.float32),
        lax.psum_scatter(
            hid_term.astype(jnp.bfloat16), "mp", scatter_dimension=1, tiled=True
        ).astype(jnp.float32),
    )
    zero_rows = jnp.zeros((tail_rows, out_cols.shape[1]), jnp.float32)
    output = jnp.concatenate([zero_rows, out_cols[:keep_rows]], 0)
    grad_hidden = jnp.concatenate([zero_rows, hid_cols[:keep_rows]], 0)
    neigh_term = contract(d_keys, wk_full) + contract(d_values, wv_full)
    neigh_cols = lax.psum_scatter(
        neigh_term.astype(jnp.bfloat16), "mp", scatter_dimension=1, tiled=True
    ).astype(jnp.float32)
    grad_neighbours = neigh_cols.reshape(blocks_here, 1, RET, neigh_cols.shape[1])
    return (output, grad_hidden, grad_neighbours)


def solution(mesh):
    return jax.shard_map(
        per_device,
        mesh=mesh,
        in_specs=(
            P("dp", "mp"),
            P("dp", "group", None),
            P("dp"),
            P(("dp", "group"), "mp"),
            P("group", "mp"),
            P("group", "mp"),
            P("group", "mp"),
            P("mp", "group"),
            P("dp", "mp"),
        ),
        out_specs=(P("dp", "mp"), P("dp", "mp"), P("dp", "group", None, "mp")),
        check_vma=False,
    )
```

```python
import math

import jax
import jax.numpy as jnp
from jax import lax
from jax.sharding import PartitionSpec as P

HD = 128
BLOCK = 64
RET = 128


def contract(left, right):
    return lax.dot_general(
        left, right, (((1,), (1,)), ((), ())), preferred_element_type=jnp.float32
    )


def per_device(
    hidden, neighbour_ids, counts, embed_table, w_query, w_key, w_value, w_out, grad_out
):
    tail_rows = BLOCK - 1
    rows_here = hidden.shape[0]
    blocks_here = rows_here // BLOCK
    heads_here = w_query.shape[1] // HD
    inv_root = 1.0 / math.sqrt(HD)
    keep_rows = rows_here - tail_rows
    half = w_query.shape[0]
    me_group = lax.axis_index("group")
    me_dp = lax.axis_index("dp")
    swap = [(0, 1), (1, 0)]
    pad_rows = jnp.zeros((tail_rows, hidden.shape[1]), jnp.bfloat16)
    query_rows = jnp.concatenate([hidden[tail_rows:], pad_rows], 0)
    grad_rows = jnp.concatenate([grad_out[tail_rows:], pad_rows], 0)
    full_query, full_grad = (
        lax.all_gather(query_rows, "mp", axis=1, tiled=True),
        lax.all_gather(grad_rows, "mp", axis=1, tiled=True),
    )
    piece_rows = half // lax.axis_size("dp")
    kv_local = jnp.concatenate([w_key, w_value], axis=1)
    kv_piece = lax.dynamic_slice_in_dim(kv_local, me_dp * piece_rows, piece_rows, 0)
    kv_other = lax.all_gather(
        lax.ppermute(kv_piece, "group", swap), "dp", axis=0, tiled=True
    )
    cols_kv = w_key.shape[1]
    wk_other, wv_other = kv_other[:, :cols_kv], kv_other[:, cols_kv:]

    flat_ids = neighbour_ids.reshape(-1)
    block_rows = embed_table.shape[0]
    owners = lax.axis_size("dp") * lax.axis_size("group")
    cap = flat_ids.shape[0] // 4
    ids_f = lax.all_gather(flat_ids.astype(jnp.float32), "group", axis=0)
    every_id = lax.all_gather(ids_f, "dp", axis=0).astype(jnp.int32).reshape(owners, -1)
    owner = me_dp * lax.axis_size("group") + me_group
    local_ids = every_id - owner * block_rows
    inside = (local_ids >= 0) & (local_ids < block_rows)
    rank = jnp.cumsum(inside.astype(jnp.int32), axis=1) - 1
    slot_hit = inside[:, :, None] & (rank[:, :, None] == jnp.arange(cap)[None, None, :])
    send_rows = jnp.sum(jnp.where(slot_hit, local_ids[:, :, None], 0), axis=1)
    send_buf = embed_table[send_rows.reshape(-1)].reshape(owners, cap, -1)
    recv_buf = lax.all_to_all(send_buf, ("dp", "group"), 0, 0, tiled=True)
    own_owner = flat_ids // block_rows
    same_owner = own_owner[:, None] == jnp.arange(owners)[None, :]
    own_rank = jnp.sum(
        jnp.where(same_owner, jnp.cumsum(same_owner.astype(jnp.int32), axis=0), 0), axis=1
    ) - 1
    own_cols = recv_buf.reshape(owners * cap, -1)[own_owner * cap + own_rank]
    neighbours = lax.all_gather(own_cols, "mp", axis=1, tiled=True)

    def this_half(x):
        return lax.dynamic_slice_in_dim(x, me_group * half, half, 1)

    def other_half(x):
        return lax.dynamic_slice_in_dim(x, (1 - me_group) * half, half, 1)

    query_part = jnp.dot(this_half(full_query), w_query, preferred_element_type=jnp.float32)
    query = lax.psum(query_part, "group").astype(jnp.bfloat16)
    n_here, n_there = this_half(neighbours), other_half(neighbours)
    keys = (
        jnp.dot(n_here, w_key, preferred_element_type=jnp.float32)
        + jnp.dot(n_there, wk_other, preferred_element_type=jnp.float32)
    ).astype(jnp.bfloat16)
    values = (
        jnp.dot(n_here, w_value, preferred_element_type=jnp.float32)
        + jnp.dot(n_there, wv_other, preferred_element_type=jnp.float32)
    ).astype(jnp.bfloat16)
    key_block = keys.reshape(blocks_here, RET, heads_here, HD)
    value_block = values.reshape(blocks_here, RET, heads_here, HD)
    query_block = query.reshape(blocks_here, BLOCK, heads_here, HD)
    live = (counts > me_group).astype(jnp.float32)
    scores = (
        jnp.einsum("cqhd,ckhd->chqk", query_block, key_block, preferred_element_type=jnp.float32)
        * inv_root
    )
    weights = jnp.exp(scores) * live[:, None, None, None]
    numer = jnp.einsum(
        "chqk,ckhd->cqhd",
        weights.astype(jnp.bfloat16),
        value_block,
        preferred_element_type=jnp.float32,
    )
    partial_total = jnp.sum(weights, -1)
    numer, partial_total = lax.psum((numer, partial_total), "group")
    total = partial_total + 1.0
    attn = numer / jnp.transpose(total, (0, 2, 1))[..., None]
    attn_bf = attn.reshape(rows_here, heads_here * HD).astype(jnp.bfloat16)

    def place_half(x):
        zeros = jnp.zeros_like(x)
        return jnp.where(
            me_group == 0, jnp.concatenate([x, zeros], 1), jnp.concatenate([zeros, x], 1)
        )

    out_term = jnp.dot(attn_bf, w_out, preferred_element_type=jnp.float32)
    d_attn_part = contract(this_half(full_grad), w_out)
    d_attn = lax.psum(d_attn_part, "group").astype(jnp.bfloat16)
    d_block = d_attn.reshape(blocks_here, BLOCK, heads_here, HD)
    prob = weights / total[..., None]
    d_prob = jnp.einsum("cqhd,ckhd->chqk", d_block, value_block, preferred_element_type=jnp.float32)
    delta = jnp.sum(d_block.astype(jnp.float32) * attn, -1)
    d_score = (prob * (d_prob - jnp.transpose(delta, (0, 2, 1))[..., None])).astype(jnp.bfloat16)
    query_part = jnp.einsum(
        "chqk,ckhd->cqhd", d_score, key_block, preferred_element_type=jnp.float32
    )
    query_grad = lax.psum(query_part, "group")
    d_query = (query_grad * inv_root).astype(jnp.bfloat16).reshape(rows_here, heads_here * HD)
    d_keys = (
        jnp.einsum("chqk,cqhd->ckhd", d_score, query_block, preferred_element_type=jnp.float32)
        * inv_root
    ).astype(jnp.bfloat16)
    d_values = jnp.einsum(
        "chqk,cqhd->ckhd", prob.astype(jnp.bfloat16), d_block, preferred_element_type=jnp.float32
    ).astype(jnp.bfloat16)
    d_keys = d_keys.reshape(blocks_here * RET, heads_here * HD)
    d_values = d_values.reshape(blocks_here * RET, heads_here * HD)
    hid_term = contract(d_query, w_query)
    out_cols, hid_cols = (
        lax.psum_scatter(
            place_half(out_term.astype(jnp.bfloat16)), "mp", scatter_dimension=1, tiled=True
        ).astype(jnp.float32),
        lax.psum_scatter(
            place_half(hid_term.astype(jnp.bfloat16)), "mp", scatter_dimension=1, tiled=True
        ).astype(jnp.float32),
    )
    out_cols, hid_cols = lax.psum((out_cols, hid_cols), "group")
    zero_rows = jnp.zeros((tail_rows, out_cols.shape[1]), jnp.float32)
    output = jnp.concatenate([zero_rows, out_cols[:keep_rows]], 0)
    grad_hidden = jnp.concatenate([zero_rows, hid_cols[:keep_rows]], 0)
    term_here = contract(d_keys, w_key) + contract(d_values, w_value)
    term_there = contract(d_keys, wk_other) + contract(d_values, wv_other)
    neigh_term = jnp.where(
        me_group == 0,
        jnp.concatenate([term_here, term_there], 1),
        jnp.concatenate([term_there, term_here], 1),
    )
    neigh_cols = lax.psum_scatter(
        neigh_term.astype(jnp.bfloat16), "mp", scatter_dimension=1, tiled=True
    ).astype(jnp.float32)
    grad_neighbours = neigh_cols.reshape(blocks_here, 1, RET, neigh_cols.shape[1])
    return (output, grad_hidden, grad_neighbours)


def solution(mesh):
    return jax.shard_map(
        per_device,
        mesh=mesh,
        in_specs=(
            P("dp", "mp"),
            P("dp", "group", None),
            P("dp"),
            P(("dp", "group"), "mp"),
            P("group", "mp"),
            P("group", "mp"),
            P("group", "mp"),
            P("mp", "group"),
            P("dp", "mp"),
        ),
        out_specs=(P("dp", "mp"), P("dp", "mp"), P("dp", "group", None, "mp")),
        check_vma=False,
    )
```

```python
import math

import jax
import jax.numpy as jnp
from jax import lax
from jax.sharding import PartitionSpec as P

HD = 128
BLOCK = 64
RET = 128


def contract(left, right):
    return lax.dot_general(
        left, right, (((1,), (1,)), ((), ())), preferred_element_type=jnp.float32
    )


def per_device(
    hidden, neighbour_ids, counts, embed_table, w_query, w_key, w_value, w_out, grad_out
):
    tail_rows = BLOCK - 1
    rows_here = hidden.shape[0]
    blocks_here = rows_here // BLOCK
    heads_here = w_query.shape[1] // HD
    inv_root = 1.0 / math.sqrt(HD)
    keep_rows = rows_here - tail_rows
    half = w_query.shape[0]
    me_group = lax.axis_index("group")
    me_dp = lax.axis_index("dp")
    swap = [(0, 1), (1, 0)]

    def group_sum(x):
        return x + lax.ppermute(x, "group", swap)

    pad_rows = jnp.zeros((tail_rows, hidden.shape[1]), jnp.bfloat16)
    query_rows = jnp.concatenate([hidden[tail_rows:], pad_rows], 0)
    grad_rows = jnp.concatenate([grad_out[tail_rows:], pad_rows], 0)
    full_query, full_grad = (
        lax.all_gather(query_rows, "mp", axis=1, tiled=True),
        lax.all_gather(grad_rows, "mp", axis=1, tiled=True),
    )
    piece_rows = half // lax.axis_size("dp")
    kv_local = jnp.concatenate([w_key, w_value], axis=1)
    kv_piece = lax.dynamic_slice_in_dim(kv_local, me_dp * piece_rows, piece_rows, 0)
    kv_other = lax.all_gather(
        lax.ppermute(kv_piece, "group", swap), "dp", axis=0, tiled=True
    )
    cols_kv = w_key.shape[1]
    wk_other, wv_other = kv_other[:, :cols_kv], kv_other[:, cols_kv:]

    flat_ids = neighbour_ids.reshape(-1)
    block_rows = embed_table.shape[0]
    owners = lax.axis_size("dp") * lax.axis_size("group")
    cap = flat_ids.shape[0] // 4
    ids_f = lax.all_gather(flat_ids.astype(jnp.float32), "group", axis=0)
    every_id = lax.all_gather(ids_f, "dp", axis=0).astype(jnp.int32).reshape(owners, -1)
    owner = me_dp * lax.axis_size("group") + me_group
    local_ids = every_id - owner * block_rows
    inside = (local_ids >= 0) & (local_ids < block_rows)
    rank = jnp.cumsum(inside.astype(jnp.int32), axis=1) - 1
    slot_hit = inside[:, :, None] & (rank[:, :, None] == jnp.arange(cap)[None, None, :])
    send_rows = jnp.sum(jnp.where(slot_hit, local_ids[:, :, None], 0), axis=1)
    send_buf = embed_table[send_rows.reshape(-1)].reshape(owners, cap, -1)
    recv_buf = lax.all_to_all(send_buf, ("dp", "group"), 0, 0, tiled=True)
    own_owner = flat_ids // block_rows
    same_owner = own_owner[:, None] == jnp.arange(owners)[None, :]
    own_rank = jnp.sum(
        jnp.where(same_owner, jnp.cumsum(same_owner.astype(jnp.int32), axis=0), 0), axis=1
    ) - 1
    own_cols = recv_buf.reshape(owners * cap, -1)[own_owner * cap + own_rank]
    neighbours = lax.all_gather(own_cols, "mp", axis=1, tiled=True)

    def this_half(x):
        return lax.dynamic_slice_in_dim(x, me_group * half, half, 1)

    def other_half(x):
        return lax.dynamic_slice_in_dim(x, (1 - me_group) * half, half, 1)

    query_part = jnp.dot(this_half(full_query), w_query, preferred_element_type=jnp.float32)
    query = group_sum(query_part).astype(jnp.bfloat16)
    n_here, n_there = this_half(neighbours), other_half(neighbours)
    keys = (
        jnp.dot(n_here, w_key, preferred_element_type=jnp.float32)
        + jnp.dot(n_there, wk_other, preferred_element_type=jnp.float32)
    ).astype(jnp.bfloat16)
    values = (
        jnp.dot(n_here, w_value, preferred_element_type=jnp.float32)
        + jnp.dot(n_there, wv_other, preferred_element_type=jnp.float32)
    ).astype(jnp.bfloat16)
    key_block = keys.reshape(blocks_here, RET, heads_here, HD)
    value_block = values.reshape(blocks_here, RET, heads_here, HD)
    query_block = query.reshape(blocks_here, BLOCK, heads_here, HD)
    live = (counts > me_group).astype(jnp.float32)
    scores = (
        jnp.einsum("cqhd,ckhd->chqk", query_block, key_block, preferred_element_type=jnp.float32)
        * inv_root
    )
    weights = jnp.exp(scores) * live[:, None, None, None]
    numer = jnp.einsum(
        "chqk,ckhd->cqhd",
        weights.astype(jnp.bfloat16),
        value_block,
        preferred_element_type=jnp.float32,
    )
    partial_total = jnp.sum(weights, -1)
    numer, partial_total = group_sum(numer), group_sum(partial_total)
    total = partial_total + 1.0
    attn = numer / jnp.transpose(total, (0, 2, 1))[..., None]
    attn_bf = attn.reshape(rows_here, heads_here * HD).astype(jnp.bfloat16)

    def place_half(x):
        zeros = jnp.zeros_like(x)
        return jnp.where(
            me_group == 0, jnp.concatenate([x, zeros], 1), jnp.concatenate([zeros, x], 1)
        )

    out_term = jnp.dot(attn_bf, w_out, preferred_element_type=jnp.float32)
    d_attn_part = contract(this_half(full_grad), w_out)
    d_attn = group_sum(d_attn_part).astype(jnp.bfloat16)
    d_block = d_attn.reshape(blocks_here, BLOCK, heads_here, HD)
    prob = weights / total[..., None]
    d_prob = jnp.einsum("cqhd,ckhd->chqk", d_block, value_block, preferred_element_type=jnp.float32)
    delta = jnp.sum(d_block.astype(jnp.float32) * attn, -1)
    d_score = (prob * (d_prob - jnp.transpose(delta, (0, 2, 1))[..., None])).astype(jnp.bfloat16)
    query_part = jnp.einsum(
        "chqk,ckhd->cqhd", d_score, key_block, preferred_element_type=jnp.float32
    )
    query_grad = group_sum(query_part)
    d_query = (query_grad * inv_root).astype(jnp.bfloat16).reshape(rows_here, heads_here * HD)
    d_keys = (
        jnp.einsum("chqk,cqhd->ckhd", d_score, query_block, preferred_element_type=jnp.float32)
        * inv_root
    ).astype(jnp.bfloat16)
    d_values = jnp.einsum(
        "chqk,cqhd->ckhd", prob.astype(jnp.bfloat16), d_block, preferred_element_type=jnp.float32
    ).astype(jnp.bfloat16)
    d_keys = d_keys.reshape(blocks_here * RET, heads_here * HD)
    d_values = d_values.reshape(blocks_here * RET, heads_here * HD)
    hid_term = contract(d_query, w_query)
    term_here = contract(d_keys, w_key) + contract(d_values, w_value)
    term_there = contract(d_keys, wk_other) + contract(d_values, wv_other)
    neigh_term = jnp.where(
        me_group == 0,
        jnp.concatenate([term_here, term_there], 1),
        jnp.concatenate([term_there, term_here], 1),
    )
    stacked = jnp.concatenate(
        [
            place_half(out_term.astype(jnp.bfloat16)),
            place_half(hid_term.astype(jnp.bfloat16)),
            neigh_term.astype(jnp.bfloat16),
        ],
        0,
    )
    reduced = lax.psum_scatter(stacked, "mp", scatter_dimension=1, tiled=True)
    both_cols = reduced[: 2 * rows_here]
    both_cols = (both_cols + lax.ppermute(both_cols, "group", swap)).astype(jnp.float32)
    out_cols, hid_cols = both_cols[:rows_here], both_cols[rows_here:]
    zero_rows = jnp.zeros((tail_rows, out_cols.shape[1]), jnp.float32)
    output = jnp.concatenate([zero_rows, out_cols[:keep_rows]], 0)
    grad_hidden = jnp.concatenate([zero_rows, hid_cols[:keep_rows]], 0)
    neigh_cols = reduced[2 * rows_here :].astype(jnp.float32)
    grad_neighbours = neigh_cols.reshape(blocks_here, 1, RET, neigh_cols.shape[1])
    return (output, grad_hidden, grad_neighbours)


def solution(mesh):
    return jax.shard_map(
        per_device,
        mesh=mesh,
        in_specs=(
            P("dp", "mp"),
            P("dp", "group", None),
            P("dp"),
            P(("dp", "group"), "mp"),
            P("group", "mp"),
            P("group", "mp"),
            P("group", "mp"),
            P("mp", "group"),
            P("dp", "mp"),
        ),
        out_specs=(P("dp", "mp"), P("dp", "mp"), P("dp", "group", None, "mp")),
        check_vma=False,
    )
```

```python
import math

import jax
import jax.numpy as jnp
from jax import lax
from jax.sharding import PartitionSpec as P

HD = 128
BLOCK = 64
RET = 128


def contract(left, right):
    return lax.dot_general(
        left, right, (((1,), (1,)), ((), ())), preferred_element_type=jnp.float32
    )


def per_device(
    hidden, neighbour_ids, counts, embed_table, w_query, w_key, w_value, w_out, grad_out
):
    tail_rows = BLOCK - 1
    rows_here = hidden.shape[0]
    blocks_here = rows_here // BLOCK
    heads_here = w_query.shape[1] // HD
    inv_root = 1.0 / math.sqrt(HD)
    keep_rows = rows_here - tail_rows
    half = w_query.shape[0]
    me_group = lax.axis_index("group")
    me_dp = lax.axis_index("dp")
    swap = [(0, 1), (1, 0)]

    def group_sum(x):
        return x + lax.ppermute(x, "group", swap)

    pad_rows = jnp.zeros((tail_rows, hidden.shape[1]), jnp.bfloat16)
    query_rows = jnp.concatenate([hidden[tail_rows:], pad_rows], 0)
    grad_rows = jnp.concatenate([grad_out[tail_rows:], pad_rows], 0)
    full_query, full_grad = (
        lax.all_gather(query_rows, "mp", axis=1, tiled=True),
        lax.all_gather(grad_rows, "mp", axis=1, tiled=True),
    )
    flat_ids = neighbour_ids.reshape(-1)
    n_ids = flat_ids.shape[0]
    block_rows = embed_table.shape[0]
    owners = lax.axis_size("dp") * lax.axis_size("group")
    cap = n_ids // 4
    piece_rows = half // lax.axis_size("dp")
    kv_local = jnp.concatenate([w_key, w_value], axis=1)
    width_kv = kv_local.shape[1]
    kv_piece = lax.dynamic_slice_in_dim(kv_local, me_dp * piece_rows, piece_rows, 0)

    def id_row(ids):
        row = jnp.concatenate([ids // 256, ids % 256]).astype(jnp.bfloat16)
        return jnp.pad(row, (0, width_kv - row.shape[0]))[None, :]

    tail_pad = jnp.zeros((7, width_kv), jnp.bfloat16)
    mine_row = id_row(flat_ids)
    got = lax.ppermute(jnp.concatenate([kv_piece, mine_row, tail_pad], 0), "group", swap)
    partner_row = got[piece_rows : piece_rows + 1]
    pair_rows = jnp.where(
        me_group == 0,
        jnp.concatenate([mine_row, partner_row], 0),
        jnp.concatenate([partner_row, mine_row], 0),
    )
    shared = jnp.concatenate([got[:piece_rows], pair_rows, tail_pad[:6]], 0)
    gathered = lax.all_gather(shared, "dp", axis=0)
    kv_other = gathered[:, :piece_rows].reshape(-1, width_kv)
    cols_kv = w_key.shape[1]
    wk_other, wv_other = kv_other[:, :cols_kv], kv_other[:, cols_kv:]
    id_bytes = gathered[:, piece_rows : piece_rows + 2, : 2 * n_ids].astype(jnp.int32)
    id_bytes = id_bytes.reshape(owners, 2, n_ids)
    every_id = id_bytes[:, 0] * 256 + id_bytes[:, 1]
    owner = me_dp * lax.axis_size("group") + me_group
    local_ids = every_id - owner * block_rows
    inside = (local_ids >= 0) & (local_ids < block_rows)
    rank = jnp.cumsum(inside.astype(jnp.int32), axis=1) - 1
    slot_hit = inside[:, :, None] & (rank[:, :, None] == jnp.arange(cap)[None, None, :])
    send_rows = jnp.sum(jnp.where(slot_hit, local_ids[:, :, None], 0), axis=1)
    send_buf = embed_table[send_rows.reshape(-1)].reshape(owners, cap, -1)
    recv_buf = lax.all_to_all(send_buf, ("dp", "group"), 0, 0, tiled=True)
    own_owner = flat_ids // block_rows
    same_owner = own_owner[:, None] == jnp.arange(owners)[None, :]
    own_rank = jnp.sum(
        jnp.where(same_owner, jnp.cumsum(same_owner.astype(jnp.int32), axis=0), 0), axis=1
    ) - 1
    own_cols = recv_buf.reshape(owners * cap, -1)[own_owner * cap + own_rank]
    neighbours = lax.all_gather(own_cols, "mp", axis=1, tiled=True)

    def this_half(x):
        return lax.dynamic_slice_in_dim(x, me_group * half, half, 1)

    def other_half(x):
        return lax.dynamic_slice_in_dim(x, (1 - me_group) * half, half, 1)

    query_part = jnp.dot(this_half(full_query), w_query, preferred_element_type=jnp.float32)
    query = group_sum(query_part).astype(jnp.bfloat16)
    n_here, n_there = this_half(neighbours), other_half(neighbours)
    keys = (
        jnp.dot(n_here, w_key, preferred_element_type=jnp.float32)
        + jnp.dot(n_there, wk_other, preferred_element_type=jnp.float32)
    ).astype(jnp.bfloat16)
    values = (
        jnp.dot(n_here, w_value, preferred_element_type=jnp.float32)
        + jnp.dot(n_there, wv_other, preferred_element_type=jnp.float32)
    ).astype(jnp.bfloat16)
    key_block = keys.reshape(blocks_here, RET, heads_here, HD)
    value_block = values.reshape(blocks_here, RET, heads_here, HD)
    query_block = query.reshape(blocks_here, BLOCK, heads_here, HD)
    live = (counts > me_group).astype(jnp.float32)
    scores = (
        jnp.einsum("cqhd,ckhd->chqk", query_block, key_block, preferred_element_type=jnp.float32)
        * inv_root
    )
    weights = jnp.exp(scores) * live[:, None, None, None]
    numer = jnp.einsum(
        "chqk,ckhd->cqhd",
        weights.astype(jnp.bfloat16),
        value_block,
        preferred_element_type=jnp.float32,
    )
    partial_total = jnp.sum(weights, -1)
    numer, partial_total = group_sum(numer), group_sum(partial_total)
    total = partial_total + 1.0
    attn = numer / jnp.transpose(total, (0, 2, 1))[..., None]
    attn_bf = attn.reshape(rows_here, heads_here * HD).astype(jnp.bfloat16)

    def place_half(x):
        zeros = jnp.zeros_like(x)
        return jnp.where(
            me_group == 0, jnp.concatenate([x, zeros], 1), jnp.concatenate([zeros, x], 1)
        )

    out_term = jnp.dot(attn_bf, w_out, preferred_element_type=jnp.float32)
    d_attn_part = contract(this_half(full_grad), w_out)
    d_attn = group_sum(d_attn_part).astype(jnp.bfloat16)
    d_block = d_attn.reshape(blocks_here, BLOCK, heads_here, HD)
    prob = weights / total[..., None]
    d_prob = jnp.einsum("cqhd,ckhd->chqk", d_block, value_block, preferred_element_type=jnp.float32)
    delta = jnp.sum(d_block.astype(jnp.float32) * attn, -1)
    d_score = (prob * (d_prob - jnp.transpose(delta, (0, 2, 1))[..., None])).astype(jnp.bfloat16)
    query_part = jnp.einsum(
        "chqk,ckhd->cqhd", d_score, key_block, preferred_element_type=jnp.float32
    )
    query_grad = group_sum(query_part)
    d_query = (query_grad * inv_root).astype(jnp.bfloat16).reshape(rows_here, heads_here * HD)
    d_keys = (
        jnp.einsum("chqk,cqhd->ckhd", d_score, query_block, preferred_element_type=jnp.float32)
        * inv_root
    ).astype(jnp.bfloat16)
    d_values = jnp.einsum(
        "chqk,cqhd->ckhd", prob.astype(jnp.bfloat16), d_block, preferred_element_type=jnp.float32
    ).astype(jnp.bfloat16)
    d_keys = d_keys.reshape(blocks_here * RET, heads_here * HD)
    d_values = d_values.reshape(blocks_here * RET, heads_here * HD)
    hid_term = contract(d_query, w_query)
    term_here = contract(d_keys, w_key) + contract(d_values, w_value)
    term_there = contract(d_keys, wk_other) + contract(d_values, wv_other)
    neigh_term = jnp.where(
        me_group == 0,
        jnp.concatenate([term_here, term_there], 1),
        jnp.concatenate([term_there, term_here], 1),
    )
    stacked = jnp.concatenate(
        [
            place_half(out_term.astype(jnp.bfloat16)),
            place_half(hid_term.astype(jnp.bfloat16)),
            neigh_term.astype(jnp.bfloat16),
        ],
        0,
    )
    reduced = lax.psum_scatter(stacked, "mp", scatter_dimension=1, tiled=True)
    both_cols = reduced[: 2 * rows_here]
    both_cols = (both_cols + lax.ppermute(both_cols, "group", swap)).astype(jnp.float32)
    out_cols, hid_cols = both_cols[:rows_here], both_cols[rows_here:]
    zero_rows = jnp.zeros((tail_rows, out_cols.shape[1]), jnp.float32)
    output = jnp.concatenate([zero_rows, out_cols[:keep_rows]], 0)
    grad_hidden = jnp.concatenate([zero_rows, hid_cols[:keep_rows]], 0)
    neigh_cols = reduced[2 * rows_here :].astype(jnp.float32)
    grad_neighbours = neigh_cols.reshape(blocks_here, 1, RET, neigh_cols.shape[1])
    return (output, grad_hidden, grad_neighbours)


def solution(mesh):
    return jax.shard_map(
        per_device,
        mesh=mesh,
        in_specs=(
            P("dp", "mp"),
            P("dp", "group", None),
            P("dp"),
            P(("dp", "group"), "mp"),
            P("group", "mp"),
            P("group", "mp"),
            P("group", "mp"),
            P("mp", "group"),
            P("dp", "mp"),
        ),
        out_specs=(P("dp", "mp"), P("dp", "mp"), P("dp", "group", None, "mp")),
        check_vma=False,
    )
```

```python
import math

import jax
import jax.numpy as jnp
from jax import lax
from jax.sharding import PartitionSpec as P

HD = 128
BLOCK = 64
RET = 128


def contract(left, right):
    return lax.dot_general(
        left, right, (((1,), (1,)), ((), ())), preferred_element_type=jnp.float32
    )


def per_device(
    hidden, neighbour_ids, counts, embed_table, w_query, w_key, w_value, w_out, grad_out
):
    tail_rows = BLOCK - 1
    rows_here = hidden.shape[0]
    blocks_here = rows_here // BLOCK
    heads_here = w_query.shape[1] // HD
    inv_root = 1.0 / math.sqrt(HD)
    keep_rows = rows_here - tail_rows
    half = w_query.shape[0]
    me_group = lax.axis_index("group")
    me_dp = lax.axis_index("dp")
    swap = [(0, 1), (1, 0)]

    def group_sum(x):
        return x + lax.ppermute(x, "group", swap)

    pad_rows = jnp.zeros((tail_rows, hidden.shape[1]), jnp.bfloat16)
    query_rows = jnp.concatenate([hidden[tail_rows:], pad_rows], 0)
    grad_rows = jnp.concatenate([grad_out[tail_rows:], pad_rows], 0)
    full_query = lax.all_gather(query_rows, "mp", axis=1, tiled=True)
    piece_rows = half // lax.axis_size("dp")
    kv_local = jnp.concatenate([w_key, w_value], axis=1)
    kv_piece = lax.dynamic_slice_in_dim(kv_local, me_dp * piece_rows, piece_rows, 0)
    kv_other = lax.all_gather(
        lax.ppermute(kv_piece, "group", swap), "dp", axis=0, tiled=True
    )
    cols_kv = w_key.shape[1]
    wk_other, wv_other = kv_other[:, :cols_kv], kv_other[:, cols_kv:]

    flat_ids = neighbour_ids.reshape(-1)
    block_rows = embed_table.shape[0]
    owners = lax.axis_size("dp") * lax.axis_size("group")
    cap = flat_ids.shape[0] // 4
    ids_f = lax.all_gather(flat_ids.astype(jnp.float32), "group", axis=0)
    every_id = lax.all_gather(ids_f, "dp", axis=0).astype(jnp.int32).reshape(owners, -1)
    owner = me_dp * lax.axis_size("group") + me_group
    local_ids = every_id - owner * block_rows
    inside = (local_ids >= 0) & (local_ids < block_rows)
    rank = jnp.cumsum(inside.astype(jnp.int32), axis=1) - 1
    slot_hit = inside[:, :, None] & (rank[:, :, None] == jnp.arange(cap)[None, None, :])
    send_rows = jnp.sum(jnp.where(slot_hit, local_ids[:, :, None], 0), axis=1)
    send_buf = embed_table[send_rows.reshape(-1)].reshape(owners, cap, -1)
    recv_buf = lax.all_to_all(send_buf, ("dp", "group"), 0, 0, tiled=True)
    own_owner = flat_ids // block_rows
    same_owner = own_owner[:, None] == jnp.arange(owners)[None, :]
    own_rank = jnp.sum(
        jnp.where(same_owner, jnp.cumsum(same_owner.astype(jnp.int32), axis=0), 0), axis=1
    ) - 1
    own_cols = recv_buf.reshape(owners * cap, -1)[own_owner * cap + own_rank]
    neighbours = lax.all_gather(own_cols, "mp", axis=1, tiled=True)
    grad_rows, neighbours = lax.optimization_barrier((grad_rows, neighbours))
    full_grad = lax.all_gather(grad_rows, "mp", axis=1, tiled=True)

    def this_half(x):
        return lax.dynamic_slice_in_dim(x, me_group * half, half, 1)

    def other_half(x):
        return lax.dynamic_slice_in_dim(x, (1 - me_group) * half, half, 1)

    query_part = jnp.dot(this_half(full_query), w_query, preferred_element_type=jnp.float32)
    query = group_sum(query_part).astype(jnp.bfloat16)
    n_here, n_there = this_half(neighbours), other_half(neighbours)
    keys = (
        jnp.dot(n_here, w_key, preferred_element_type=jnp.float32)
        + jnp.dot(n_there, wk_other, preferred_element_type=jnp.float32)
    ).astype(jnp.bfloat16)
    values = (
        jnp.dot(n_here, w_value, preferred_element_type=jnp.float32)
        + jnp.dot(n_there, wv_other, preferred_element_type=jnp.float32)
    ).astype(jnp.bfloat16)
    key_block = keys.reshape(blocks_here, RET, heads_here, HD)
    value_block = values.reshape(blocks_here, RET, heads_here, HD)
    query_block = query.reshape(blocks_here, BLOCK, heads_here, HD)
    live = (counts > me_group).astype(jnp.float32)
    scores = (
        jnp.einsum("cqhd,ckhd->chqk", query_block, key_block, preferred_element_type=jnp.float32)
        * inv_root
    )
    weights = jnp.exp(scores) * live[:, None, None, None]
    numer = jnp.einsum(
        "chqk,ckhd->cqhd",
        weights.astype(jnp.bfloat16),
        value_block,
        preferred_element_type=jnp.float32,
    )
    partial_total = jnp.sum(weights, -1)
    numer, partial_total = group_sum(numer), group_sum(partial_total)
    total = partial_total + 1.0
    attn = numer / jnp.transpose(total, (0, 2, 1))[..., None]
    attn_bf = attn.reshape(rows_here, heads_here * HD).astype(jnp.bfloat16)

    def place_half(x):
        zeros = jnp.zeros_like(x)
        return jnp.where(
            me_group == 0, jnp.concatenate([x, zeros], 1), jnp.concatenate([zeros, x], 1)
        )

    out_term = jnp.dot(attn_bf, w_out, preferred_element_type=jnp.float32)
    d_attn_part = contract(this_half(full_grad), w_out)
    d_attn = group_sum(d_attn_part).astype(jnp.bfloat16)
    d_block = d_attn.reshape(blocks_here, BLOCK, heads_here, HD)
    prob = weights / total[..., None]
    d_prob = jnp.einsum("cqhd,ckhd->chqk", d_block, value_block, preferred_element_type=jnp.float32)
    delta = jnp.sum(d_block.astype(jnp.float32) * attn, -1)
    d_score = (prob * (d_prob - jnp.transpose(delta, (0, 2, 1))[..., None])).astype(jnp.bfloat16)
    query_part = jnp.einsum(
        "chqk,ckhd->cqhd", d_score, key_block, preferred_element_type=jnp.float32
    )
    query_grad = group_sum(query_part)
    d_query = (query_grad * inv_root).astype(jnp.bfloat16).reshape(rows_here, heads_here * HD)
    d_keys = (
        jnp.einsum("chqk,cqhd->ckhd", d_score, query_block, preferred_element_type=jnp.float32)
        * inv_root
    ).astype(jnp.bfloat16)
    d_values = jnp.einsum(
        "chqk,cqhd->ckhd", prob.astype(jnp.bfloat16), d_block, preferred_element_type=jnp.float32
    ).astype(jnp.bfloat16)
    d_keys = d_keys.reshape(blocks_here * RET, heads_here * HD)
    d_values = d_values.reshape(blocks_here * RET, heads_here * HD)
    hid_term = contract(d_query, w_query)
    term_here = contract(d_keys, w_key) + contract(d_values, w_value)
    term_there = contract(d_keys, wk_other) + contract(d_values, wv_other)
    neigh_term = jnp.where(
        me_group == 0,
        jnp.concatenate([term_here, term_there], 1),
        jnp.concatenate([term_there, term_here], 1),
    )
    stacked = jnp.concatenate(
        [
            place_half(out_term.astype(jnp.bfloat16)),
            place_half(hid_term.astype(jnp.bfloat16)),
            neigh_term.astype(jnp.bfloat16),
        ],
        0,
    )
    reduced = lax.psum_scatter(stacked, "mp", scatter_dimension=1, tiled=True)
    both_cols = reduced[: 2 * rows_here]
    both_cols = (both_cols + lax.ppermute(both_cols, "group", swap)).astype(jnp.float32)
    out_cols, hid_cols = both_cols[:rows_here], both_cols[rows_here:]
    zero_rows = jnp.zeros((tail_rows, out_cols.shape[1]), jnp.float32)
    output = jnp.concatenate([zero_rows, out_cols[:keep_rows]], 0)
    grad_hidden = jnp.concatenate([zero_rows, hid_cols[:keep_rows]], 0)
    neigh_cols = reduced[2 * rows_here :].astype(jnp.float32)
    grad_neighbours = neigh_cols.reshape(blocks_here, 1, RET, neigh_cols.shape[1])
    return (output, grad_hidden, grad_neighbours)


def solution(mesh):
    return jax.shard_map(
        per_device,
        mesh=mesh,
        in_specs=(
            P("dp", "mp"),
            P("dp", "group", None),
            P("dp"),
            P(("dp", "group"), "mp"),
            P("group", "mp"),
            P("group", "mp"),
            P("group", "mp"),
            P("mp", "group"),
            P("dp", "mp"),
        ),
        out_specs=(P("dp", "mp"), P("dp", "mp"), P("dp", "group", None, "mp")),
        check_vma=False,
    )
```

```python
import functools
import math

import jax
import jax.numpy as jnp
from jax import lax
from jax.experimental import pallas as pl
from jax.experimental.pallas import tpu as pltpu
from jax.sharding import PartitionSpec as P

HD = 128
BLOCK = 64
RET = 128


def contract(left, right):
    return lax.dot_general(
        left, right, (((1,), (1,)), ((), ())), preferred_element_type=jnp.float32
    )


MESH = pl.DeviceIdType.MESH


def _half_rows_kernel(n_mp, rows_ref, out_ref, held, send_sem, recv_sem):
    me_dp = lax.axis_index("dp")
    me_mp = lax.axis_index("mp")
    me_group = lax.axis_index("group")
    half_blocks = n_mp // 2
    barrier = pltpu.get_barrier_semaphore()
    for off in range(1, n_mp):
        peer = lax.rem(me_mp + off, n_mp)
        pl.semaphore_signal(
            barrier, inc=1, device_id=(me_dp, peer, me_group), device_id_type=MESH
        )
    pl.semaphore_wait(barrier, n_mp - 1)
    slot = lax.rem(me_mp, half_blocks)
    sender = lax.div(me_mp, half_blocks) == me_group

    def copy_to(off):
        return pltpu.make_async_remote_copy(
            src_ref=rows_ref,
            dst_ref=held.at[slot],
            send_sem=send_sem.at[off - 1],
            recv_sem=recv_sem.at[slot],
            device_id=(me_dp, lax.rem(me_mp + off, n_mp), me_group),
            device_id_type=MESH,
        )

    @pl.when(sender)
    def _():
        for off in range(1, n_mp):
            copy_to(off).start()
        held[slot] = rows_ref[...]

    for s in range(half_blocks):
        source = half_blocks * me_group + s

        @pl.when(source != me_mp)
        def _():
            pltpu.make_async_remote_copy(
                src_ref=rows_ref,
                dst_ref=held.at[s],
                send_sem=send_sem.at[0],
                recv_sem=recv_sem.at[s],
                device_id=(me_dp, source, me_group),
                device_id_type=MESH,
            ).wait_recv()

    @pl.when(sender)
    def _():
        for off in range(1, n_mp):
            copy_to(off).wait_send()

    out_ref[...] = held[...]


def half_rows_exchange(rows, n_mp):
    half_blocks = n_mp // 2
    shape = (half_blocks,) + rows.shape
    moved = rows.size * rows.dtype.itemsize * (n_mp - 1)
    return pl.pallas_call(
        functools.partial(_half_rows_kernel, n_mp),
        out_shape=jax.ShapeDtypeStruct(shape, rows.dtype),
        in_specs=[pl.BlockSpec(memory_space=pltpu.VMEM)],
        out_specs=pl.BlockSpec(memory_space=pltpu.VMEM),
        scratch_shapes=[
            pltpu.VMEM(shape, rows.dtype),
            pltpu.SemaphoreType.DMA((n_mp - 1,)),
            pltpu.SemaphoreType.DMA((half_blocks,)),
        ],
        compiler_params=pltpu.CompilerParams(collective_id=0, has_side_effects=True),
        cost_estimate=pl.CostEstimate(
            flops=0, transcendentals=0, bytes_accessed=moved
        ),
    )(rows)


def per_device(
    hidden, neighbour_ids, counts, embed_table, w_query, w_key, w_value, w_out, grad_out, n_mp
):
    tail_rows = BLOCK - 1
    rows_here = hidden.shape[0]
    blocks_here = rows_here // BLOCK
    heads_here = w_query.shape[1] // HD
    inv_root = 1.0 / math.sqrt(HD)
    keep_rows = rows_here - tail_rows
    half = w_query.shape[0]
    me_group = lax.axis_index("group")
    me_dp = lax.axis_index("dp")
    swap = [(0, 1), (1, 0)]

    def group_sum(x):
        return x + lax.ppermute(x, "group", swap)

    pad_rows = jnp.zeros((tail_rows, hidden.shape[1]), jnp.bfloat16)
    query_rows = jnp.concatenate([hidden[tail_rows:], pad_rows], 0)
    grad_rows = jnp.concatenate([grad_out[tail_rows:], pad_rows], 0)
    halves = half_rows_exchange(jnp.stack([query_rows, grad_rows]), n_mp)
    halves = jnp.transpose(halves, (1, 2, 0, 3)).reshape(2, rows_here, half)
    query_half, grad_half = halves[0], halves[1]
    piece_rows = half // lax.axis_size("dp")
    kv_local = jnp.concatenate([w_key, w_value], axis=1)
    kv_piece = lax.dynamic_slice_in_dim(kv_local, me_dp * piece_rows, piece_rows, 0)
    kv_other = lax.all_gather(
        lax.ppermute(kv_piece, "group", swap), "dp", axis=0, tiled=True
    )
    cols_kv = w_key.shape[1]
    wk_other, wv_other = kv_other[:, :cols_kv], kv_other[:, cols_kv:]

    flat_ids = neighbour_ids.reshape(-1)
    block_rows = embed_table.shape[0]
    owners = lax.axis_size("dp") * lax.axis_size("group")
    cap = flat_ids.shape[0] // 4
    ids_f = lax.all_gather(flat_ids.astype(jnp.float32), "group", axis=0)
    every_id = lax.all_gather(ids_f, "dp", axis=0).astype(jnp.int32).reshape(owners, -1)
    owner = me_dp * lax.axis_size("group") + me_group
    local_ids = every_id - owner * block_rows
    inside = (local_ids >= 0) & (local_ids < block_rows)
    rank = jnp.cumsum(inside.astype(jnp.int32), axis=1) - 1
    slot_hit = inside[:, :, None] & (rank[:, :, None] == jnp.arange(cap)[None, None, :])
    send_rows = jnp.sum(jnp.where(slot_hit, local_ids[:, :, None], 0), axis=1)
    send_buf = embed_table[send_rows.reshape(-1)].reshape(owners, cap, -1)
    recv_buf = lax.all_to_all(send_buf, ("dp", "group"), 0, 0, tiled=True)
    own_owner = flat_ids // block_rows
    same_owner = own_owner[:, None] == jnp.arange(owners)[None, :]
    own_rank = jnp.sum(
        jnp.where(same_owner, jnp.cumsum(same_owner.astype(jnp.int32), axis=0), 0), axis=1
    ) - 1
    own_cols = recv_buf.reshape(owners * cap, -1)[own_owner * cap + own_rank]
    neighbours = lax.all_gather(own_cols, "mp", axis=1, tiled=True)

    def this_half(x):
        return lax.dynamic_slice_in_dim(x, me_group * half, half, 1)

    def other_half(x):
        return lax.dynamic_slice_in_dim(x, (1 - me_group) * half, half, 1)

    query_part = jnp.dot(query_half, w_query, preferred_element_type=jnp.float32)
    query = group_sum(query_part).astype(jnp.bfloat16)
    n_here, n_there = this_half(neighbours), other_half(neighbours)
    keys = (
        jnp.dot(n_here, w_key, preferred_element_type=jnp.float32)
        + jnp.dot(n_there, wk_other, preferred_element_type=jnp.float32)
    ).astype(jnp.bfloat16)
    values = (
        jnp.dot(n_here, w_value, preferred_element_type=jnp.float32)
        + jnp.dot(n_there, wv_other, preferred_element_type=jnp.float32)
    ).astype(jnp.bfloat16)
    key_block = keys.reshape(blocks_here, RET, heads_here, HD)
    value_block = values.reshape(blocks_here, RET, heads_here, HD)
    query_block = query.reshape(blocks_here, BLOCK, heads_here, HD)
    live = (counts > me_group).astype(jnp.float32)
    scores = (
        jnp.einsum("cqhd,ckhd->chqk", query_block, key_block, preferred_element_type=jnp.float32)
        * inv_root
    )
    weights = jnp.exp(scores) * live[:, None, None, None]
    numer = jnp.einsum(
        "chqk,ckhd->cqhd",
        weights.astype(jnp.bfloat16),
        value_block,
        preferred_element_type=jnp.float32,
    )
    partial_total = jnp.sum(weights, -1)
    numer, partial_total = group_sum(numer), group_sum(partial_total)
    total = partial_total + 1.0
    attn = numer / jnp.transpose(total, (0, 2, 1))[..., None]
    attn_bf = attn.reshape(rows_here, heads_here * HD).astype(jnp.bfloat16)

    def place_half(x):
        zeros = jnp.zeros_like(x)
        return jnp.where(
            me_group == 0, jnp.concatenate([x, zeros], 1), jnp.concatenate([zeros, x], 1)
        )

    out_term = jnp.dot(attn_bf, w_out, preferred_element_type=jnp.float32)
    d_attn_part = contract(grad_half, w_out)
    d_attn = group_sum(d_attn_part).astype(jnp.bfloat16)
    d_block = d_attn.reshape(blocks_here, BLOCK, heads_here, HD)
    prob = weights / total[..., None]
    d_prob = jnp.einsum("cqhd,ckhd->chqk", d_block, value_block, preferred_element_type=jnp.float32)
    delta = jnp.sum(d_block.astype(jnp.float32) * attn, -1)
    d_score = (prob * (d_prob - jnp.transpose(delta, (0, 2, 1))[..., None])).astype(jnp.bfloat16)
    query_part = jnp.einsum(
        "chqk,ckhd->cqhd", d_score, key_block, preferred_element_type=jnp.float32
    )
    query_grad = group_sum(query_part)
    d_query = (query_grad * inv_root).astype(jnp.bfloat16).reshape(rows_here, heads_here * HD)
    d_keys = (
        jnp.einsum("chqk,cqhd->ckhd", d_score, query_block, preferred_element_type=jnp.float32)
        * inv_root
    ).astype(jnp.bfloat16)
    d_values = jnp.einsum(
        "chqk,cqhd->ckhd", prob.astype(jnp.bfloat16), d_block, preferred_element_type=jnp.float32
    ).astype(jnp.bfloat16)
    d_keys = d_keys.reshape(blocks_here * RET, heads_here * HD)
    d_values = d_values.reshape(blocks_here * RET, heads_here * HD)
    hid_term = contract(d_query, w_query)
    term_here = contract(d_keys, w_key) + contract(d_values, w_value)
    term_there = contract(d_keys, wk_other) + contract(d_values, wv_other)
    neigh_term = jnp.where(
        me_group == 0,
        jnp.concatenate([term_here, term_there], 1),
        jnp.concatenate([term_there, term_here], 1),
    )
    stacked = jnp.concatenate(
        [
            place_half(out_term.astype(jnp.bfloat16)),
            place_half(hid_term.astype(jnp.bfloat16)),
            neigh_term.astype(jnp.bfloat16),
        ],
        0,
    )
    reduced = lax.psum_scatter(stacked, "mp", scatter_dimension=1, tiled=True)
    both_cols = reduced[: 2 * rows_here]
    both_cols = (both_cols + lax.ppermute(both_cols, "group", swap)).astype(jnp.float32)
    out_cols, hid_cols = both_cols[:rows_here], both_cols[rows_here:]
    zero_rows = jnp.zeros((tail_rows, out_cols.shape[1]), jnp.float32)
    output = jnp.concatenate([zero_rows, out_cols[:keep_rows]], 0)
    grad_hidden = jnp.concatenate([zero_rows, hid_cols[:keep_rows]], 0)
    neigh_cols = reduced[2 * rows_here :].astype(jnp.float32)
    grad_neighbours = neigh_cols.reshape(blocks_here, 1, RET, neigh_cols.shape[1])
    return (output, grad_hidden, grad_neighbours)


def solution(mesh):
    return jax.shard_map(
        functools.partial(per_device, n_mp=mesh.shape["mp"]),
        mesh=mesh,
        in_specs=(
            P("dp", "mp"),
            P("dp", "group", None),
            P("dp"),
            P(("dp", "group"), "mp"),
            P("group", "mp"),
            P("group", "mp"),
            P("group", "mp"),
            P("mp", "group"),
            P("dp", "mp"),
        ),
        out_specs=(P("dp", "mp"), P("dp", "mp"), P("dp", "group", None, "mp")),
        check_vma=False,
    )
```

```python
import functools
import math

import jax
import jax.numpy as jnp
from jax import lax
from jax.experimental import pallas as pl
from jax.experimental.pallas import tpu as pltpu
from jax.sharding import PartitionSpec as P

HD = 128
BLOCK = 64
RET = 128


def contract(left, right):
    return lax.dot_general(
        left, right, (((1,), (1,)), ((), ())), preferred_element_type=jnp.float32
    )


MESH = pl.DeviceIdType.MESH


def _other_half_kernel(n_dp, own_ref, out_ref, send_sem, recv_sem):
    me_dp = lax.axis_index("dp")
    me_mp = lax.axis_index("mp")
    me_group = lax.axis_index("group")
    chips = n_dp // 2
    ring = 2 * chips
    z_lo = lax.div(me_dp, 2)
    core = lax.rem(me_dp, 2)
    z = me_group * chips + z_lo
    z_next = lax.rem(z + 1, ring)
    z_prev = lax.rem(z + ring - 1, ring)

    def at_z(zz, cc):
        return (lax.rem(zz, chips) * 2 + cc, me_mp, lax.div(zz, chips))

    next_dev, prev_dev = at_z(z_next, core), at_z(z_prev, core)
    sibling = (z_lo * 2 + 1 - core, me_mp, me_group)

    barrier = pltpu.get_barrier_semaphore()
    for dev in (next_dev, prev_dev, sibling):
        pl.semaphore_signal(barrier, inc=1, device_id=dev, device_id_type=MESH)
    pl.semaphore_wait(barrier, 3)

    n_pieces = out_ref.shape[0]
    rows = out_ref.shape[1]
    quarter = n_pieces // 4

    def plus_piece(k):
        return 2 * quarter + 2 * k + core

    def minus_piece(k):
        return 2 * k + core

    def chain(src, p, dev):
        return pltpu.make_async_remote_copy(
            src_ref=src,
            dst_ref=out_ref.at[p],
            send_sem=send_sem.at[p],
            recv_sem=recv_sem.at[p],
            device_id=dev,
            device_id_type=MESH,
        )

    def to_sibling(p):
        return pltpu.make_async_remote_copy(
            src_ref=out_ref.at[p],
            dst_ref=out_ref.at[p],
            send_sem=send_sem.at[n_pieces + p],
            recv_sem=recv_sem.at[p],
            device_id=sibling,
            device_id_type=MESH,
        )

    def own(p):
        return own_ref.at[pl.ds(pl.multiple_of(p * rows, rows), rows)]

    @pl.when(z_lo == chips - 1)
    def _():
        for k in range(quarter):
            p = plus_piece(k)
            chain(own(p), p, next_dev).start()

    @pl.when(z_lo == 0)
    def _():
        for k in range(quarter):
            p = minus_piece(k)
            chain(own(p), p, prev_dev).start()

    for k in range(quarter):
        for p, fwd, dev in (
            (plus_piece(k), z_lo < chips - 1, next_dev),
            (minus_piece(k), z_lo > 0, prev_dev),
        ):
            chain(out_ref.at[p], p, dev).wait_recv()

            @pl.when(fwd)
            def _():
                chain(out_ref.at[p], p, dev).start()

            to_sibling(p).start()

    for k in range(quarter):
        for p in (plus_piece(k) + 1 - 2 * core, minus_piece(k) + 1 - 2 * core):
            to_sibling(p).wait_recv()
    for k in range(quarter):
        for p in (plus_piece(k), minus_piece(k)):
            chain(out_ref.at[p], p, next_dev).wait_send()
            to_sibling(p).wait_send()


def other_half_exchange(own, n_dp):
    n_pieces = n_dp
    rows = own.shape[0] // n_pieces
    shape = (n_pieces, rows, own.shape[1])
    moved = own.size * own.dtype.itemsize
    return pl.pallas_call(
        functools.partial(_other_half_kernel, n_dp),
        out_shape=jax.ShapeDtypeStruct(shape, own.dtype),
        in_specs=[pl.BlockSpec(memory_space=pltpu.VMEM)],
        out_specs=pl.BlockSpec(memory_space=pltpu.VMEM),
        scratch_shapes=[
            pltpu.SemaphoreType.DMA((2 * n_pieces,)),
            pltpu.SemaphoreType.DMA((n_pieces,)),
        ],
        compiler_params=pltpu.CompilerParams(collective_id=0, has_side_effects=True),
        cost_estimate=pl.CostEstimate(flops=0, transcendentals=0, bytes_accessed=moved),
    )(own).reshape(own.shape)


def per_device(
    hidden, neighbour_ids, counts, embed_table, w_query, w_key, w_value, w_out, grad_out, n_dp
):
    tail_rows = BLOCK - 1
    rows_here = hidden.shape[0]
    blocks_here = rows_here // BLOCK
    heads_here = w_query.shape[1] // HD
    inv_root = 1.0 / math.sqrt(HD)
    keep_rows = rows_here - tail_rows
    half = w_query.shape[0]
    me_group = lax.axis_index("group")
    me_dp = lax.axis_index("dp")
    swap = [(0, 1), (1, 0)]

    def group_sum(x):
        return x + lax.ppermute(x, "group", swap)

    pad_rows = jnp.zeros((tail_rows, hidden.shape[1]), jnp.bfloat16)
    query_rows = jnp.concatenate([hidden[tail_rows:], pad_rows], 0)
    grad_rows = jnp.concatenate([grad_out[tail_rows:], pad_rows], 0)
    full_query, full_grad = (
        lax.all_gather(query_rows, "mp", axis=1, tiled=True),
        lax.all_gather(grad_rows, "mp", axis=1, tiled=True),
    )

    flat_ids = neighbour_ids.reshape(-1)
    block_rows = embed_table.shape[0]
    owners = lax.axis_size("dp") * lax.axis_size("group")
    cap = flat_ids.shape[0] // 4
    ids_f = lax.all_gather(flat_ids.astype(jnp.float32), "group", axis=0)
    every_id = lax.all_gather(ids_f, "dp", axis=0).astype(jnp.int32).reshape(owners, -1)
    owner = me_dp * lax.axis_size("group") + me_group
    local_ids = every_id - owner * block_rows
    inside = (local_ids >= 0) & (local_ids < block_rows)
    rank = jnp.cumsum(inside.astype(jnp.int32), axis=1) - 1
    slot_hit = inside[:, :, None] & (rank[:, :, None] == jnp.arange(cap)[None, None, :])
    send_rows = jnp.sum(jnp.where(slot_hit, local_ids[:, :, None], 0), axis=1)
    send_buf = embed_table[send_rows.reshape(-1)].reshape(owners, cap, -1)
    recv_buf = lax.all_to_all(send_buf, ("dp", "group"), 0, 0, tiled=True)
    own_owner = flat_ids // block_rows
    same_owner = own_owner[:, None] == jnp.arange(owners)[None, :]
    own_rank = jnp.sum(
        jnp.where(same_owner, jnp.cumsum(same_owner.astype(jnp.int32), axis=0), 0), axis=1
    ) - 1
    own_cols = recv_buf.reshape(owners * cap, -1)[own_owner * cap + own_rank]
    neighbours = lax.all_gather(own_cols, "mp", axis=1, tiled=True)
    kv_local = jnp.concatenate([w_key, w_value], axis=1)
    kv_local, own_cols = lax.optimization_barrier((kv_local, own_cols))
    kv_other = other_half_exchange(kv_local, n_dp)
    cols_kv = w_key.shape[1]
    wk_other, wv_other = kv_other[:, :cols_kv], kv_other[:, cols_kv:]

    def this_half(x):
        return lax.dynamic_slice_in_dim(x, me_group * half, half, 1)

    def other_half(x):
        return lax.dynamic_slice_in_dim(x, (1 - me_group) * half, half, 1)

    query_part = jnp.dot(this_half(full_query), w_query, preferred_element_type=jnp.float32)
    query = group_sum(query_part).astype(jnp.bfloat16)
    n_here, n_there = this_half(neighbours), other_half(neighbours)
    keys = (
        jnp.dot(n_here, w_key, preferred_element_type=jnp.float32)
        + jnp.dot(n_there, wk_other, preferred_element_type=jnp.float32)
    ).astype(jnp.bfloat16)
    values = (
        jnp.dot(n_here, w_value, preferred_element_type=jnp.float32)
        + jnp.dot(n_there, wv_other, preferred_element_type=jnp.float32)
    ).astype(jnp.bfloat16)
    key_block = keys.reshape(blocks_here, RET, heads_here, HD)
    value_block = values.reshape(blocks_here, RET, heads_here, HD)
    query_block = query.reshape(blocks_here, BLOCK, heads_here, HD)
    live = (counts > me_group).astype(jnp.float32)
    scores = (
        jnp.einsum("cqhd,ckhd->chqk", query_block, key_block, preferred_element_type=jnp.float32)
        * inv_root
    )
    weights = jnp.exp(scores) * live[:, None, None, None]
    numer = jnp.einsum(
        "chqk,ckhd->cqhd",
        weights.astype(jnp.bfloat16),
        value_block,
        preferred_element_type=jnp.float32,
    )
    partial_total = jnp.sum(weights, -1)
    numer, partial_total = group_sum(numer), group_sum(partial_total)
    total = partial_total + 1.0
    attn = numer / jnp.transpose(total, (0, 2, 1))[..., None]
    attn_bf = attn.reshape(rows_here, heads_here * HD).astype(jnp.bfloat16)

    def place_half(x):
        zeros = jnp.zeros_like(x)
        return jnp.where(
            me_group == 0, jnp.concatenate([x, zeros], 1), jnp.concatenate([zeros, x], 1)
        )

    out_term = jnp.dot(attn_bf, w_out, preferred_element_type=jnp.float32)
    d_attn_part = contract(this_half(full_grad), w_out)
    d_attn = group_sum(d_attn_part).astype(jnp.bfloat16)
    d_block = d_attn.reshape(blocks_here, BLOCK, heads_here, HD)
    prob = weights / total[..., None]
    d_prob = jnp.einsum("cqhd,ckhd->chqk", d_block, value_block, preferred_element_type=jnp.float32)
    delta = jnp.sum(d_block.astype(jnp.float32) * attn, -1)
    d_score = (prob * (d_prob - jnp.transpose(delta, (0, 2, 1))[..., None])).astype(jnp.bfloat16)
    query_part = jnp.einsum(
        "chqk,ckhd->cqhd", d_score, key_block, preferred_element_type=jnp.float32
    )
    query_grad = group_sum(query_part)
    d_query = (query_grad * inv_root).astype(jnp.bfloat16).reshape(rows_here, heads_here * HD)
    d_keys = (
        jnp.einsum("chqk,cqhd->ckhd", d_score, query_block, preferred_element_type=jnp.float32)
        * inv_root
    ).astype(jnp.bfloat16)
    d_values = jnp.einsum(
        "chqk,cqhd->ckhd", prob.astype(jnp.bfloat16), d_block, preferred_element_type=jnp.float32
    ).astype(jnp.bfloat16)
    d_keys = d_keys.reshape(blocks_here * RET, heads_here * HD)
    d_values = d_values.reshape(blocks_here * RET, heads_here * HD)
    hid_term = contract(d_query, w_query)
    term_here = contract(d_keys, w_key) + contract(d_values, w_value)
    term_there = contract(d_keys, wk_other) + contract(d_values, wv_other)
    neigh_term = jnp.where(
        me_group == 0,
        jnp.concatenate([term_here, term_there], 1),
        jnp.concatenate([term_there, term_here], 1),
    )
    stacked = jnp.concatenate(
        [
            place_half(out_term.astype(jnp.bfloat16)),
            place_half(hid_term.astype(jnp.bfloat16)),
            neigh_term.astype(jnp.bfloat16),
        ],
        0,
    )
    reduced = lax.psum_scatter(stacked, "mp", scatter_dimension=1, tiled=True)
    both_cols = reduced[: 2 * rows_here]
    both_cols = (both_cols + lax.ppermute(both_cols, "group", swap)).astype(jnp.float32)
    out_cols, hid_cols = both_cols[:rows_here], both_cols[rows_here:]
    zero_rows = jnp.zeros((tail_rows, out_cols.shape[1]), jnp.float32)
    output = jnp.concatenate([zero_rows, out_cols[:keep_rows]], 0)
    grad_hidden = jnp.concatenate([zero_rows, hid_cols[:keep_rows]], 0)
    neigh_cols = reduced[2 * rows_here :].astype(jnp.float32)
    grad_neighbours = neigh_cols.reshape(blocks_here, 1, RET, neigh_cols.shape[1])
    return (output, grad_hidden, grad_neighbours)


def solution(mesh):
    return jax.shard_map(
        functools.partial(per_device, n_dp=mesh.shape["dp"]),
        mesh=mesh,
        in_specs=(
            P("dp", "mp"),
            P("dp", "group", None),
            P("dp"),
            P(("dp", "group"), "mp"),
            P("group", "mp"),
            P("group", "mp"),
            P("group", "mp"),
            P("mp", "group"),
            P("dp", "mp"),
        ),
        out_specs=(P("dp", "mp"), P("dp", "mp"), P("dp", "group", None, "mp")),
        check_vma=False,
    )
```

```python
import functools
import math

import jax
import jax.numpy as jnp
from jax import lax
from jax.experimental import pallas as pl
from jax.experimental.pallas import tpu as pltpu
from jax.sharding import PartitionSpec as P

HD = 128
BLOCK = 64
RET = 128


def contract(left, right):
    return lax.dot_general(
        left, right, (((1,), (1,)), ((), ())), preferred_element_type=jnp.float32
    )


MESH = pl.DeviceIdType.MESH


def _other_half_kernel(n_dp, own_ref, out_ref, send_sem, recv_sem):
    me_dp = lax.axis_index("dp")
    me_mp = lax.axis_index("mp")
    me_group = lax.axis_index("group")
    chips = n_dp // 2
    ring = 2 * chips
    z_lo = lax.div(me_dp, 2)
    core = lax.rem(me_dp, 2)
    z = me_group * chips + z_lo
    z_next = lax.rem(z + 1, ring)
    z_prev = lax.rem(z + ring - 1, ring)

    def at_z(zz, cc):
        return (lax.rem(zz, chips) * 2 + cc, me_mp, lax.div(zz, chips))

    next_dev, prev_dev = at_z(z_next, core), at_z(z_prev, core)
    sibling = (z_lo * 2 + 1 - core, me_mp, me_group)

    barrier = pltpu.get_barrier_semaphore()
    for dev in (next_dev, prev_dev, sibling):
        pl.semaphore_signal(barrier, inc=1, device_id=dev, device_id_type=MESH)
    pl.semaphore_wait(barrier, 3)

    n_pieces = out_ref.shape[0]
    rows = out_ref.shape[1]
    quarter = n_pieces // 4

    def plus_piece(k):
        return 2 * quarter + 2 * k + core

    def minus_piece(k):
        return 2 * k + core

    def chain(src, p, dev):
        return pltpu.make_async_remote_copy(
            src_ref=src,
            dst_ref=out_ref.at[p],
            send_sem=send_sem.at[p],
            recv_sem=recv_sem.at[p],
            device_id=dev,
            device_id_type=MESH,
        )

    def to_sibling(p):
        return pltpu.make_async_remote_copy(
            src_ref=out_ref.at[p],
            dst_ref=out_ref.at[p],
            send_sem=send_sem.at[n_pieces + p],
            recv_sem=recv_sem.at[p],
            device_id=sibling,
            device_id_type=MESH,
        )

    def own(p):
        return own_ref.at[pl.ds(pl.multiple_of(p * rows, rows), rows)]

    @pl.when(z_lo == chips - 1)
    def _():
        for k in range(quarter):
            p = plus_piece(k)
            chain(own(p), p, next_dev).start()

    @pl.when(z_lo == 0)
    def _():
        for k in range(quarter):
            p = minus_piece(k)
            chain(own(p), p, prev_dev).start()

    for k in range(quarter):
        for p, fwd, dev in (
            (plus_piece(k), z_lo < chips - 1, next_dev),
            (minus_piece(k), z_lo > 0, prev_dev),
        ):
            chain(out_ref.at[p], p, dev).wait_recv()

            @pl.when(fwd)
            def _():
                chain(out_ref.at[p], p, dev).start()

            to_sibling(p).start()

    for k in range(quarter):
        for p in (plus_piece(k) + 1 - 2 * core, minus_piece(k) + 1 - 2 * core):
            to_sibling(p).wait_recv()
    for k in range(quarter):
        for p in (plus_piece(k), minus_piece(k)):
            chain(out_ref.at[p], p, next_dev).wait_send()
            to_sibling(p).wait_send()


def other_half_exchange(own, n_dp):
    n_pieces = 2 * n_dp
    rows = own.shape[0] // n_pieces
    shape = (n_pieces, rows, own.shape[1])
    moved = own.size * own.dtype.itemsize
    return pl.pallas_call(
        functools.partial(_other_half_kernel, n_dp),
        out_shape=jax.ShapeDtypeStruct(shape, own.dtype),
        in_specs=[pl.BlockSpec(memory_space=pltpu.VMEM)],
        out_specs=pl.BlockSpec(memory_space=pltpu.VMEM),
        scratch_shapes=[
            pltpu.SemaphoreType.DMA((2 * n_pieces,)),
            pltpu.SemaphoreType.DMA((n_pieces,)),
        ],
        compiler_params=pltpu.CompilerParams(collective_id=0, has_side_effects=True),
        cost_estimate=pl.CostEstimate(flops=0, transcendentals=0, bytes_accessed=moved),
    )(own).reshape(own.shape)


def per_device(
    hidden, neighbour_ids, counts, embed_table, w_query, w_key, w_value, w_out, grad_out, n_dp
):
    tail_rows = BLOCK - 1
    rows_here = hidden.shape[0]
    blocks_here = rows_here // BLOCK
    heads_here = w_query.shape[1] // HD
    inv_root = 1.0 / math.sqrt(HD)
    keep_rows = rows_here - tail_rows
    half = w_query.shape[0]
    me_group = lax.axis_index("group")
    me_dp = lax.axis_index("dp")
    swap = [(0, 1), (1, 0)]

    def group_sum(x):
        return x + lax.ppermute(x, "group", swap)

    pad_rows = jnp.zeros((tail_rows, hidden.shape[1]), jnp.bfloat16)
    query_rows = jnp.concatenate([hidden[tail_rows:], pad_rows], 0)
    grad_rows = jnp.concatenate([grad_out[tail_rows:], pad_rows], 0)
    full_query, full_grad = (
        lax.all_gather(query_rows, "mp", axis=1, tiled=True),
        lax.all_gather(grad_rows, "mp", axis=1, tiled=True),
    )

    flat_ids = neighbour_ids.reshape(-1)
    block_rows = embed_table.shape[0]
    owners = lax.axis_size("dp") * lax.axis_size("group")
    cap = flat_ids.shape[0] // 4
    ids_f = lax.all_gather(flat_ids.astype(jnp.float32), "group", axis=0)
    every_id = lax.all_gather(ids_f, "dp", axis=0).astype(jnp.int32).reshape(owners, -1)
    owner = me_dp * lax.axis_size("group") + me_group
    local_ids = every_id - owner * block_rows
    inside = (local_ids >= 0) & (local_ids < block_rows)
    rank = jnp.cumsum(inside.astype(jnp.int32), axis=1) - 1
    slot_hit = inside[:, :, None] & (rank[:, :, None] == jnp.arange(cap)[None, None, :])
    send_rows = jnp.sum(jnp.where(slot_hit, local_ids[:, :, None], 0), axis=1)
    send_buf = embed_table[send_rows.reshape(-1)].reshape(owners, cap, -1)
    recv_buf = lax.all_to_all(send_buf, ("dp", "group"), 0, 0, tiled=True)
    own_owner = flat_ids // block_rows
    same_owner = own_owner[:, None] == jnp.arange(owners)[None, :]
    own_rank = jnp.sum(
        jnp.where(same_owner, jnp.cumsum(same_owner.astype(jnp.int32), axis=0), 0), axis=1
    ) - 1
    own_cols = recv_buf.reshape(owners * cap, -1)[own_owner * cap + own_rank]
    neighbours = lax.all_gather(own_cols, "mp", axis=1, tiled=True)
    kv_local = jnp.concatenate([w_key, w_value], axis=1)
    kv_local, own_cols = lax.optimization_barrier((kv_local, own_cols))
    kv_other = other_half_exchange(kv_local, n_dp)
    cols_kv = w_key.shape[1]
    wk_other, wv_other = kv_other[:, :cols_kv], kv_other[:, cols_kv:]

    def this_half(x):
        return lax.dynamic_slice_in_dim(x, me_group * half, half, 1)

    def other_half(x):
        return lax.dynamic_slice_in_dim(x, (1 - me_group) * half, half, 1)

    query_part = jnp.dot(this_half(full_query), w_query, preferred_element_type=jnp.float32)
    query = group_sum(query_part).astype(jnp.bfloat16)
    n_here, n_there = this_half(neighbours), other_half(neighbours)
    keys = (
        jnp.dot(n_here, w_key, preferred_element_type=jnp.float32)
        + jnp.dot(n_there, wk_other, preferred_element_type=jnp.float32)
    ).astype(jnp.bfloat16)
    values = (
        jnp.dot(n_here, w_value, preferred_element_type=jnp.float32)
        + jnp.dot(n_there, wv_other, preferred_element_type=jnp.float32)
    ).astype(jnp.bfloat16)
    key_block = keys.reshape(blocks_here, RET, heads_here, HD)
    value_block = values.reshape(blocks_here, RET, heads_here, HD)
    query_block = query.reshape(blocks_here, BLOCK, heads_here, HD)
    live = (counts > me_group).astype(jnp.float32)
    scores = (
        jnp.einsum("cqhd,ckhd->chqk", query_block, key_block, preferred_element_type=jnp.float32)
        * inv_root
    )
    weights = jnp.exp(scores) * live[:, None, None, None]
    numer = jnp.einsum(
        "chqk,ckhd->cqhd",
        weights.astype(jnp.bfloat16),
        value_block,
        preferred_element_type=jnp.float32,
    )
    partial_total = jnp.sum(weights, -1)
    numer, partial_total = group_sum(numer), group_sum(partial_total)
    total = partial_total + 1.0
    attn = numer / jnp.transpose(total, (0, 2, 1))[..., None]
    attn_bf = attn.reshape(rows_here, heads_here * HD).astype(jnp.bfloat16)

    def place_half(x):
        zeros = jnp.zeros_like(x)
        return jnp.where(
            me_group == 0, jnp.concatenate([x, zeros], 1), jnp.concatenate([zeros, x], 1)
        )

    out_term = jnp.dot(attn_bf, w_out, preferred_element_type=jnp.float32)
    d_attn_part = contract(this_half(full_grad), w_out)
    d_attn = group_sum(d_attn_part).astype(jnp.bfloat16)
    d_block = d_attn.reshape(blocks_here, BLOCK, heads_here, HD)
    prob = weights / total[..., None]
    d_prob = jnp.einsum("cqhd,ckhd->chqk", d_block, value_block, preferred_element_type=jnp.float32)
    delta = jnp.sum(d_block.astype(jnp.float32) * attn, -1)
    d_score = (prob * (d_prob - jnp.transpose(delta, (0, 2, 1))[..., None])).astype(jnp.bfloat16)
    query_part = jnp.einsum(
        "chqk,ckhd->cqhd", d_score, key_block, preferred_element_type=jnp.float32
    )
    query_grad = group_sum(query_part)
    d_query = (query_grad * inv_root).astype(jnp.bfloat16).reshape(rows_here, heads_here * HD)
    d_keys = (
        jnp.einsum("chqk,cqhd->ckhd", d_score, query_block, preferred_element_type=jnp.float32)
        * inv_root
    ).astype(jnp.bfloat16)
    d_values = jnp.einsum(
        "chqk,cqhd->ckhd", prob.astype(jnp.bfloat16), d_block, preferred_element_type=jnp.float32
    ).astype(jnp.bfloat16)
    d_keys = d_keys.reshape(blocks_here * RET, heads_here * HD)
    d_values = d_values.reshape(blocks_here * RET, heads_here * HD)
    hid_term = contract(d_query, w_query)
    term_here = contract(d_keys, w_key) + contract(d_values, w_value)
    term_there = contract(d_keys, wk_other) + contract(d_values, wv_other)
    neigh_term = jnp.where(
        me_group == 0,
        jnp.concatenate([term_here, term_there], 1),
        jnp.concatenate([term_there, term_here], 1),
    )
    stacked = jnp.concatenate(
        [
            place_half(out_term.astype(jnp.bfloat16)),
            place_half(hid_term.astype(jnp.bfloat16)),
            neigh_term.astype(jnp.bfloat16),
        ],
        0,
    )
    reduced = lax.psum_scatter(stacked, "mp", scatter_dimension=1, tiled=True)
    both_cols = reduced[: 2 * rows_here]
    both_cols = (both_cols + lax.ppermute(both_cols, "group", swap)).astype(jnp.float32)
    out_cols, hid_cols = both_cols[:rows_here], both_cols[rows_here:]
    zero_rows = jnp.zeros((tail_rows, out_cols.shape[1]), jnp.float32)
    output = jnp.concatenate([zero_rows, out_cols[:keep_rows]], 0)
    grad_hidden = jnp.concatenate([zero_rows, hid_cols[:keep_rows]], 0)
    neigh_cols = reduced[2 * rows_here :].astype(jnp.float32)
    grad_neighbours = neigh_cols.reshape(blocks_here, 1, RET, neigh_cols.shape[1])
    return (output, grad_hidden, grad_neighbours)


def solution(mesh):
    return jax.shard_map(
        functools.partial(per_device, n_dp=mesh.shape["dp"]),
        mesh=mesh,
        in_specs=(
            P("dp", "mp"),
            P("dp", "group", None),
            P("dp"),
            P(("dp", "group"), "mp"),
            P("group", "mp"),
            P("group", "mp"),
            P("group", "mp"),
            P("mp", "group"),
            P("dp", "mp"),
        ),
        out_specs=(P("dp", "mp"), P("dp", "mp"), P("dp", "group", None, "mp")),
        check_vma=False,
    )
```

```python
import functools
import math

import jax
import jax.numpy as jnp
from jax import lax
from jax.experimental import pallas as pl
from jax.experimental.pallas import tpu as pltpu
from jax.sharding import PartitionSpec as P

HD = 128
BLOCK = 64
RET = 128


def contract(left, right):
    return lax.dot_general(
        left, right, (((1,), (1,)), ((), ())), preferred_element_type=jnp.float32
    )


MESH = pl.DeviceIdType.MESH


def _other_half_kernel(n_dp, own_ref, out_ref, send_sem, recv_sem):
    me_dp = lax.axis_index("dp")
    me_mp = lax.axis_index("mp")
    me_group = lax.axis_index("group")
    chips = n_dp // 2
    ring = 2 * chips
    z_lo = lax.div(me_dp, 2)
    core = lax.rem(me_dp, 2)
    z = me_group * chips + z_lo
    z_next = lax.rem(z + 1, ring)
    z_prev = lax.rem(z + ring - 1, ring)

    def at_z(zz, cc):
        return (lax.rem(zz, chips) * 2 + cc, me_mp, lax.div(zz, chips))

    next_dev, prev_dev = at_z(z_next, core), at_z(z_prev, core)
    sibling = (z_lo * 2 + 1 - core, me_mp, me_group)

    barrier = pltpu.get_barrier_semaphore()
    for dev in (next_dev, prev_dev, sibling):
        pl.semaphore_signal(barrier, inc=1, device_id=dev, device_id_type=MESH)
    pl.semaphore_wait(barrier, 3)

    n_pieces = out_ref.shape[0]
    rows = out_ref.shape[1]
    quarter = n_pieces // 4

    def plus_piece(k):
        return 2 * quarter + 2 * k + core

    def minus_piece(k):
        return 2 * k + core

    def chain(src, p, dev):
        return pltpu.make_async_remote_copy(
            src_ref=src,
            dst_ref=out_ref.at[p],
            send_sem=send_sem.at[p],
            recv_sem=recv_sem.at[p],
            device_id=dev,
            device_id_type=MESH,
        )

    def to_sibling(p):
        return pltpu.make_async_remote_copy(
            src_ref=out_ref.at[p],
            dst_ref=out_ref.at[p],
            send_sem=send_sem.at[n_pieces + p],
            recv_sem=recv_sem.at[p],
            device_id=sibling,
            device_id_type=MESH,
        )

    def own(p):
        return own_ref.at[pl.ds(pl.multiple_of(p * rows, rows), rows)]

    @pl.when(z_lo == chips - 1)
    def _():
        for k in range(quarter):
            p = plus_piece(k)
            chain(own(p), p, next_dev).start()

    @pl.when(z_lo == 0)
    def _():
        for k in range(quarter):
            p = minus_piece(k)
            chain(own(p), p, prev_dev).start()

    for k in range(quarter):
        for p, fwd, dev in (
            (plus_piece(k), z_lo < chips - 1, next_dev),
            (minus_piece(k), z_lo > 0, prev_dev),
        ):
            chain(out_ref.at[p], p, dev).wait_recv()

            @pl.when(fwd)
            def _():
                chain(out_ref.at[p], p, dev).start()

            to_sibling(p).start()

    for k in range(quarter):
        for p in (plus_piece(k) + 1 - 2 * core, minus_piece(k) + 1 - 2 * core):
            to_sibling(p).wait_recv()
    for k in range(quarter):
        for p in (plus_piece(k), minus_piece(k)):
            chain(out_ref.at[p], p, next_dev).wait_send()
            to_sibling(p).wait_send()


def other_half_exchange(own, n_dp):
    n_pieces = n_dp
    rows = own.shape[0] // n_pieces
    shape = (n_pieces, rows, own.shape[1])
    moved = own.size * own.dtype.itemsize
    return pl.pallas_call(
        functools.partial(_other_half_kernel, n_dp),
        out_shape=jax.ShapeDtypeStruct(shape, own.dtype),
        in_specs=[pl.BlockSpec(memory_space=pltpu.VMEM)],
        out_specs=pl.BlockSpec(memory_space=pltpu.VMEM),
        scratch_shapes=[
            pltpu.SemaphoreType.DMA((2 * n_pieces,)),
            pltpu.SemaphoreType.DMA((n_pieces,)),
        ],
        compiler_params=pltpu.CompilerParams(collective_id=0, has_side_effects=True),
        cost_estimate=pl.CostEstimate(flops=0, transcendentals=0, bytes_accessed=moved),
    )(own).reshape(own.shape)


def per_device(
    hidden, neighbour_ids, counts, embed_table, w_query, w_key, w_value, w_out, grad_out, n_dp
):
    tail_rows = BLOCK - 1
    rows_here = hidden.shape[0]
    blocks_here = rows_here // BLOCK
    heads_here = w_query.shape[1] // HD
    inv_root = 1.0 / math.sqrt(HD)
    keep_rows = rows_here - tail_rows
    half = w_query.shape[0]
    me_group = lax.axis_index("group")
    me_dp = lax.axis_index("dp")
    swap = [(0, 1), (1, 0)]

    def group_sum(x):
        return x + lax.ppermute(x, "group", swap)

    pad_rows = jnp.zeros((tail_rows, hidden.shape[1]), jnp.bfloat16)
    query_rows = jnp.concatenate([hidden[tail_rows:], pad_rows], 0)
    grad_rows = jnp.concatenate([grad_out[tail_rows:], pad_rows], 0)
    full_query, full_grad = (
        lax.all_gather(query_rows, "mp", axis=1, tiled=True),
        lax.all_gather(grad_rows, "mp", axis=1, tiled=True),
    )

    flat_ids = neighbour_ids.reshape(-1)
    block_rows = embed_table.shape[0]
    owners = lax.axis_size("dp") * lax.axis_size("group")
    cap = flat_ids.shape[0] // 4
    ids_out = jnp.broadcast_to(flat_ids.astype(jnp.float32)[None], (owners, flat_ids.shape[0]))
    every_id = lax.all_to_all(ids_out, ("dp", "group"), 0, 0, tiled=True).astype(jnp.int32)
    owner = me_dp * lax.axis_size("group") + me_group
    local_ids = every_id - owner * block_rows
    inside = (local_ids >= 0) & (local_ids < block_rows)
    rank = jnp.cumsum(inside.astype(jnp.int32), axis=1) - 1
    slot_hit = inside[:, :, None] & (rank[:, :, None] == jnp.arange(cap)[None, None, :])
    send_rows = jnp.sum(jnp.where(slot_hit, local_ids[:, :, None], 0), axis=1)
    send_buf = embed_table[send_rows.reshape(-1)].reshape(owners, cap, -1)
    recv_buf = lax.all_to_all(send_buf, ("dp", "group"), 0, 0, tiled=True)
    own_owner = flat_ids // block_rows
    same_owner = own_owner[:, None] == jnp.arange(owners)[None, :]
    own_rank = jnp.sum(
        jnp.where(same_owner, jnp.cumsum(same_owner.astype(jnp.int32), axis=0), 0), axis=1
    ) - 1
    own_cols = recv_buf.reshape(owners * cap, -1)[own_owner * cap + own_rank]
    neighbours = lax.all_gather(own_cols, "mp", axis=1, tiled=True)
    kv_local = jnp.concatenate([w_key, w_value], axis=1)
    kv_local, own_cols = lax.optimization_barrier((kv_local, own_cols))
    kv_other = other_half_exchange(kv_local, n_dp)
    cols_kv = w_key.shape[1]
    wk_other, wv_other = kv_other[:, :cols_kv], kv_other[:, cols_kv:]

    def this_half(x):
        return lax.dynamic_slice_in_dim(x, me_group * half, half, 1)

    def other_half(x):
        return lax.dynamic_slice_in_dim(x, (1 - me_group) * half, half, 1)

    query_part = jnp.dot(this_half(full_query), w_query, preferred_element_type=jnp.float32)
    d_attn_part = contract(this_half(full_grad), w_out)
    query_sum, d_attn_sum = group_sum(jnp.stack([query_part, d_attn_part]))
    query = query_sum.astype(jnp.bfloat16)
    n_here, n_there = this_half(neighbours), other_half(neighbours)
    keys = (
        jnp.dot(n_here, w_key, preferred_element_type=jnp.float32)
        + jnp.dot(n_there, wk_other, preferred_element_type=jnp.float32)
    ).astype(jnp.bfloat16)
    values = (
        jnp.dot(n_here, w_value, preferred_element_type=jnp.float32)
        + jnp.dot(n_there, wv_other, preferred_element_type=jnp.float32)
    ).astype(jnp.bfloat16)
    key_block = keys.reshape(blocks_here, RET, heads_here, HD)
    value_block = values.reshape(blocks_here, RET, heads_here, HD)
    query_block = query.reshape(blocks_here, BLOCK, heads_here, HD)
    live = (counts > me_group).astype(jnp.float32)
    scores = (
        jnp.einsum("cqhd,ckhd->chqk", query_block, key_block, preferred_element_type=jnp.float32)
        * inv_root
    )
    weights = jnp.exp(scores) * live[:, None, None, None]
    numer = jnp.einsum(
        "chqk,ckhd->cqhd",
        weights.astype(jnp.bfloat16),
        value_block,
        preferred_element_type=jnp.float32,
    )
    partial_total = jnp.sum(weights, -1)
    numer_size = numer.size
    joined = group_sum(jnp.concatenate([numer.reshape(-1), partial_total.reshape(-1)]))
    numer = joined[:numer_size].reshape(numer.shape)
    partial_total = joined[numer_size:].reshape(partial_total.shape)
    total = partial_total + 1.0
    attn = numer / jnp.transpose(total, (0, 2, 1))[..., None]
    attn_bf = attn.reshape(rows_here, heads_here * HD).astype(jnp.bfloat16)

    def place_half(x):
        zeros = jnp.zeros_like(x)
        return jnp.where(
            me_group == 0, jnp.concatenate([x, zeros], 1), jnp.concatenate([zeros, x], 1)
        )

    out_term = jnp.dot(attn_bf, w_out, preferred_element_type=jnp.float32)
    d_attn = d_attn_sum.astype(jnp.bfloat16)
    d_block = d_attn.reshape(blocks_here, BLOCK, heads_here, HD)
    prob = weights / total[..., None]
    d_prob = jnp.einsum("cqhd,ckhd->chqk", d_block, value_block, preferred_element_type=jnp.float32)
    delta = jnp.sum(d_block.astype(jnp.float32) * attn, -1)
    d_score = (prob * (d_prob - jnp.transpose(delta, (0, 2, 1))[..., None])).astype(jnp.bfloat16)
    query_part = jnp.einsum(
        "chqk,ckhd->cqhd", d_score, key_block, preferred_element_type=jnp.float32
    )
    query_grad = group_sum(query_part)
    d_query = (query_grad * inv_root).astype(jnp.bfloat16).reshape(rows_here, heads_here * HD)
    d_keys = (
        jnp.einsum("chqk,cqhd->ckhd", d_score, query_block, preferred_element_type=jnp.float32)
        * inv_root
    ).astype(jnp.bfloat16)
    d_values = jnp.einsum(
        "chqk,cqhd->ckhd", prob.astype(jnp.bfloat16), d_block, preferred_element_type=jnp.float32
    ).astype(jnp.bfloat16)
    d_keys = d_keys.reshape(blocks_here * RET, heads_here * HD)
    d_values = d_values.reshape(blocks_here * RET, heads_here * HD)
    hid_term = contract(d_query, w_query)
    term_here = contract(d_keys, w_key) + contract(d_values, w_value)
    term_there = contract(d_keys, wk_other) + contract(d_values, wv_other)
    neigh_term = jnp.where(
        me_group == 0,
        jnp.concatenate([term_here, term_there], 1),
        jnp.concatenate([term_there, term_here], 1),
    )
    stacked = jnp.concatenate(
        [
            place_half(out_term.astype(jnp.bfloat16)),
            place_half(hid_term.astype(jnp.bfloat16)),
            neigh_term.astype(jnp.bfloat16),
        ],
        0,
    )
    reduced = lax.psum_scatter(stacked, "mp", scatter_dimension=1, tiled=True)
    both_cols = reduced[: 2 * rows_here]
    both_cols = (both_cols + lax.ppermute(both_cols, "group", swap)).astype(jnp.float32)
    out_cols, hid_cols = both_cols[:rows_here], both_cols[rows_here:]
    zero_rows = jnp.zeros((tail_rows, out_cols.shape[1]), jnp.float32)
    output = jnp.concatenate([zero_rows, out_cols[:keep_rows]], 0)
    grad_hidden = jnp.concatenate([zero_rows, hid_cols[:keep_rows]], 0)
    neigh_cols = reduced[2 * rows_here :].astype(jnp.float32)
    grad_neighbours = neigh_cols.reshape(blocks_here, 1, RET, neigh_cols.shape[1])
    return (output, grad_hidden, grad_neighbours)


def solution(mesh):
    return jax.shard_map(
        functools.partial(per_device, n_dp=mesh.shape["dp"]),
        mesh=mesh,
        in_specs=(
            P("dp", "mp"),
            P("dp", "group", None),
            P("dp"),
            P(("dp", "group"), "mp"),
            P("group", "mp"),
            P("group", "mp"),
            P("group", "mp"),
            P("mp", "group"),
            P("dp", "mp"),
        ),
        out_specs=(P("dp", "mp"), P("dp", "mp"), P("dp", "group", None, "mp")),
        check_vma=False,
    )
```

```python
import math

import jax
import jax.numpy as jnp
from jax import lax
from jax.sharding import PartitionSpec as P

HD = 128
BLOCK = 64
RET = 128


def contract(left, right):
    return lax.dot_general(
        left, right, (((1,), (1,)), ((), ())), preferred_element_type=jnp.float32
    )


def per_device(
    hidden, neighbour_ids, counts, embed_table, w_query, w_key, w_value, w_out, grad_out
):
    tail_rows = BLOCK - 1
    rows_here = hidden.shape[0]
    blocks_here = rows_here // BLOCK
    heads_here = w_query.shape[1] // HD
    inv_root = 1.0 / math.sqrt(HD)
    keep_rows = rows_here - tail_rows
    half = w_query.shape[0]
    me_group = lax.axis_index("group")
    me_dp = lax.axis_index("dp")
    swap = [(0, 1), (1, 0)]

    def group_sum(x):
        return x + lax.ppermute(x, "group", swap)

    pad_rows = jnp.zeros((tail_rows, hidden.shape[1]), jnp.bfloat16)
    query_rows = jnp.concatenate([hidden[tail_rows:], pad_rows], 0)
    grad_rows = jnp.concatenate([grad_out[tail_rows:], pad_rows], 0)
    full_query, full_grad = (
        lax.all_gather(query_rows, "mp", axis=1, tiled=True),
        lax.all_gather(grad_rows, "mp", axis=1, tiled=True),
    )
    piece_rows = half // lax.axis_size("dp")
    kv_local = jnp.concatenate([w_key, w_value], axis=1)
    kv_piece = lax.dynamic_slice_in_dim(kv_local, me_dp * piece_rows, piece_rows, 0)
    held = lax.ppermute(kv_piece, "group", swap)[None]
    n_dp = lax.axis_size("dp")
    bit = n_dp // 2
    while bit >= 1:
        pairs = [(i, i ^ bit) for i in range(n_dp)]
        other = lax.ppermute(held, "dp", pairs)
        low = (me_dp // bit) % 2 == 0
        held = jnp.where(
            low, jnp.concatenate([held, other], 0), jnp.concatenate([other, held], 0)
        )
        bit //= 2
    n_bits = n_dp.bit_length() - 1
    held = held.reshape((2,) * n_bits + held.shape[1:])
    held = jnp.transpose(held, tuple(reversed(range(n_bits))) + (n_bits, n_bits + 1))
    kv_other = held.reshape(-1, held.shape[-1])
    cols_kv = w_key.shape[1]
    wk_other, wv_other = kv_other[:, :cols_kv], kv_other[:, cols_kv:]

    flat_ids = neighbour_ids.reshape(-1)
    block_rows = embed_table.shape[0]
    owners = lax.axis_size("dp") * lax.axis_size("group")
    cap = flat_ids.shape[0] // 4
    ids_out = jnp.broadcast_to(flat_ids.astype(jnp.float32)[None], (owners, flat_ids.shape[0]))
    every_id = lax.all_to_all(ids_out, ("dp", "group"), 0, 0, tiled=True).astype(jnp.int32)
    owner = me_dp * lax.axis_size("group") + me_group
    local_ids = every_id - owner * block_rows
    inside = (local_ids >= 0) & (local_ids < block_rows)
    rank = jnp.cumsum(inside.astype(jnp.int32), axis=1) - 1
    slot_hit = inside[:, :, None] & (rank[:, :, None] == jnp.arange(cap)[None, None, :])
    send_rows = jnp.sum(jnp.where(slot_hit, local_ids[:, :, None], 0), axis=1)
    send_buf = embed_table[send_rows.reshape(-1)].reshape(owners, cap, -1)
    recv_buf = lax.all_to_all(send_buf, ("dp", "group"), 0, 0, tiled=True)
    own_owner = flat_ids // block_rows
    same_owner = own_owner[:, None] == jnp.arange(owners)[None, :]
    own_rank = jnp.sum(
        jnp.where(same_owner, jnp.cumsum(same_owner.astype(jnp.int32), axis=0), 0), axis=1
    ) - 1
    own_cols = recv_buf.reshape(owners * cap, -1)[own_owner * cap + own_rank]
    neighbours = lax.all_gather(own_cols, "mp", axis=1, tiled=True)

    def this_half(x):
        return lax.dynamic_slice_in_dim(x, me_group * half, half, 1)

    def other_half(x):
        return lax.dynamic_slice_in_dim(x, (1 - me_group) * half, half, 1)

    query_part = jnp.dot(this_half(full_query), w_query, preferred_element_type=jnp.float32)
    query = group_sum(query_part).astype(jnp.bfloat16)
    n_here, n_there = this_half(neighbours), other_half(neighbours)
    keys = (
        jnp.dot(n_here, w_key, preferred_element_type=jnp.float32)
        + jnp.dot(n_there, wk_other, preferred_element_type=jnp.float32)
    ).astype(jnp.bfloat16)
    values = (
        jnp.dot(n_here, w_value, preferred_element_type=jnp.float32)
        + jnp.dot(n_there, wv_other, preferred_element_type=jnp.float32)
    ).astype(jnp.bfloat16)
    key_block = keys.reshape(blocks_here, RET, heads_here, HD)
    value_block = values.reshape(blocks_here, RET, heads_here, HD)
    query_block = query.reshape(blocks_here, BLOCK, heads_here, HD)
    live = (counts > me_group).astype(jnp.float32)
    scores = (
        jnp.einsum("cqhd,ckhd->chqk", query_block, key_block, preferred_element_type=jnp.float32)
        * inv_root
    )
    weights = jnp.exp(scores) * live[:, None, None, None]
    numer = jnp.einsum(
        "chqk,ckhd->cqhd",
        weights.astype(jnp.bfloat16),
        value_block,
        preferred_element_type=jnp.float32,
    )
    partial_total = jnp.sum(weights, -1)
    numer, partial_total = group_sum(numer), group_sum(partial_total)
    total = partial_total + 1.0
    attn = numer / jnp.transpose(total, (0, 2, 1))[..., None]
    attn_bf = attn.reshape(rows_here, heads_here * HD).astype(jnp.bfloat16)

    def place_half(x):
        zeros = jnp.zeros_like(x)
        return jnp.where(
            me_group == 0, jnp.concatenate([x, zeros], 1), jnp.concatenate([zeros, x], 1)
        )

    out_term = jnp.dot(attn_bf, w_out, preferred_element_type=jnp.float32)
    d_attn_part = contract(this_half(full_grad), w_out)
    d_attn = group_sum(d_attn_part).astype(jnp.bfloat16)
    d_block = d_attn.reshape(blocks_here, BLOCK, heads_here, HD)
    prob = weights / total[..., None]
    d_prob = jnp.einsum("cqhd,ckhd->chqk", d_block, value_block, preferred_element_type=jnp.float32)
    delta = jnp.sum(d_block.astype(jnp.float32) * attn, -1)
    d_score = (prob * (d_prob - jnp.transpose(delta, (0, 2, 1))[..., None])).astype(jnp.bfloat16)
    query_part = jnp.einsum(
        "chqk,ckhd->cqhd", d_score, key_block, preferred_element_type=jnp.float32
    )
    query_grad = group_sum(query_part)
    d_query = (query_grad * inv_root).astype(jnp.bfloat16).reshape(rows_here, heads_here * HD)
    d_keys = (
        jnp.einsum("chqk,cqhd->ckhd", d_score, query_block, preferred_element_type=jnp.float32)
        * inv_root
    ).astype(jnp.bfloat16)
    d_values = jnp.einsum(
        "chqk,cqhd->ckhd", prob.astype(jnp.bfloat16), d_block, preferred_element_type=jnp.float32
    ).astype(jnp.bfloat16)
    d_keys = d_keys.reshape(blocks_here * RET, heads_here * HD)
    d_values = d_values.reshape(blocks_here * RET, heads_here * HD)
    hid_term = contract(d_query, w_query)
    term_here = contract(d_keys, w_key) + contract(d_values, w_value)
    term_there = contract(d_keys, wk_other) + contract(d_values, wv_other)
    neigh_term = jnp.where(
        me_group == 0,
        jnp.concatenate([term_here, term_there], 1),
        jnp.concatenate([term_there, term_here], 1),
    )
    stacked = jnp.concatenate(
        [
            place_half(out_term.astype(jnp.bfloat16)),
            place_half(hid_term.astype(jnp.bfloat16)),
            neigh_term.astype(jnp.bfloat16),
        ],
        0,
    )
    reduced = lax.psum_scatter(stacked, "mp", scatter_dimension=1, tiled=True)
    both_cols = reduced[: 2 * rows_here]
    both_cols = (both_cols + lax.ppermute(both_cols, "group", swap)).astype(jnp.float32)
    out_cols, hid_cols = both_cols[:rows_here], both_cols[rows_here:]
    zero_rows = jnp.zeros((tail_rows, out_cols.shape[1]), jnp.float32)
    output = jnp.concatenate([zero_rows, out_cols[:keep_rows]], 0)
    grad_hidden = jnp.concatenate([zero_rows, hid_cols[:keep_rows]], 0)
    neigh_cols = reduced[2 * rows_here :].astype(jnp.float32)
    grad_neighbours = neigh_cols.reshape(blocks_here, 1, RET, neigh_cols.shape[1])
    return (output, grad_hidden, grad_neighbours)


def solution(mesh):
    return jax.shard_map(
        per_device,
        mesh=mesh,
        in_specs=(
            P("dp", "mp"),
            P("dp", "group", None),
            P("dp"),
            P(("dp", "group"), "mp"),
            P("group", "mp"),
            P("group", "mp"),
            P("group", "mp"),
            P("mp", "group"),
            P("dp", "mp"),
        ),
        out_specs=(P("dp", "mp"), P("dp", "mp"), P("dp", "group", None, "mp")),
        check_vma=False,
    )
```

```python
import math

import jax
import jax.numpy as jnp
from jax import lax
from jax.sharding import PartitionSpec as P

HD = 128
BLOCK = 64
RET = 128


def contract(left, right):
    return lax.dot_general(
        left, right, (((1,), (1,)), ((), ())), preferred_element_type=jnp.float32
    )


def per_device(
    hidden, neighbour_ids, counts, embed_table, w_query, w_key, w_value, w_out, grad_out
):
    tail_rows = BLOCK - 1
    rows_here = hidden.shape[0]
    blocks_here = rows_here // BLOCK
    heads_here = w_query.shape[1] // HD
    inv_root = 1.0 / math.sqrt(HD)
    keep_rows = rows_here - tail_rows
    half = w_query.shape[0]
    me_group = lax.axis_index("group")
    me_dp = lax.axis_index("dp")
    swap = [(0, 1), (1, 0)]

    def group_sum(x):
        return x + lax.ppermute(x, "group", swap)

    pad_rows = jnp.zeros((tail_rows, hidden.shape[1]), jnp.bfloat16)
    query_rows = jnp.concatenate([hidden[tail_rows:], pad_rows], 0)
    grad_rows = jnp.concatenate([grad_out[tail_rows:], pad_rows], 0)
    n_mp = lax.axis_size("mp")
    me_mp = lax.axis_index("mp")
    rows2 = jnp.stack([query_rows, grad_rows])
    across = lax.ppermute(rows2, "mp", [(i, i ^ (n_mp // 2)) for i in range(n_mp)])
    held_rows = jnp.where(me_mp // (n_mp // 2) == me_group, rows2, across)[None]
    bit = n_mp // 4
    while bit >= 1:
        pairs = [(i, i ^ bit) for i in range(n_mp)]
        other = lax.ppermute(held_rows, "mp", pairs)
        low = (me_mp // bit) % 2 == 0
        held_rows = jnp.where(
            low,
            jnp.concatenate([held_rows, other], 0),
            jnp.concatenate([other, held_rows], 0),
        )
        bit //= 2
    m_bits = (n_mp // 2).bit_length() - 1
    held_rows = held_rows.reshape((2,) * m_bits + held_rows.shape[1:])
    held_rows = jnp.transpose(
        held_rows, (m_bits,) + tuple(reversed(range(m_bits))) + (m_bits + 1, m_bits + 2)
    )
    halves = jnp.transpose(
        held_rows.reshape((2, n_mp // 2) + held_rows.shape[-2:]), (0, 2, 1, 3)
    ).reshape(2, rows_here, half)
    query_half, grad_half = halves[0], halves[1]
    piece_rows = half // lax.axis_size("dp")
    kv_local = jnp.concatenate([w_key, w_value], axis=1)
    kv_piece = lax.dynamic_slice_in_dim(kv_local, me_dp * piece_rows, piece_rows, 0)
    held = lax.ppermute(kv_piece, "group", swap)[None]
    n_dp = lax.axis_size("dp")
    bit = n_dp // 2
    while bit >= 1:
        pairs = [(i, i ^ bit) for i in range(n_dp)]
        other = lax.ppermute(held, "dp", pairs)
        low = (me_dp // bit) % 2 == 0
        held = jnp.where(
            low, jnp.concatenate([held, other], 0), jnp.concatenate([other, held], 0)
        )
        bit //= 2
    n_bits = n_dp.bit_length() - 1
    held = held.reshape((2,) * n_bits + held.shape[1:])
    held = jnp.transpose(held, tuple(reversed(range(n_bits))) + (n_bits, n_bits + 1))
    kv_other = held.reshape(-1, held.shape[-1])
    cols_kv = w_key.shape[1]
    wk_other, wv_other = kv_other[:, :cols_kv], kv_other[:, cols_kv:]

    flat_ids = neighbour_ids.reshape(-1)
    block_rows = embed_table.shape[0]
    owners = lax.axis_size("dp") * lax.axis_size("group")
    cap = flat_ids.shape[0] // 4
    ids_out = jnp.broadcast_to(flat_ids.astype(jnp.float32)[None], (owners, flat_ids.shape[0]))
    every_id = lax.all_to_all(ids_out, ("dp", "group"), 0, 0, tiled=True).astype(jnp.int32)
    owner = me_dp * lax.axis_size("group") + me_group
    local_ids = every_id - owner * block_rows
    inside = (local_ids >= 0) & (local_ids < block_rows)
    rank = jnp.cumsum(inside.astype(jnp.int32), axis=1) - 1
    slot_hit = inside[:, :, None] & (rank[:, :, None] == jnp.arange(cap)[None, None, :])
    send_rows = jnp.sum(jnp.where(slot_hit, local_ids[:, :, None], 0), axis=1)
    send_buf = embed_table[send_rows.reshape(-1)].reshape(owners, cap, -1)
    recv_buf = lax.all_to_all(send_buf, ("dp", "group"), 0, 0, tiled=True)
    own_owner = flat_ids // block_rows
    same_owner = own_owner[:, None] == jnp.arange(owners)[None, :]
    own_rank = jnp.sum(
        jnp.where(same_owner, jnp.cumsum(same_owner.astype(jnp.int32), axis=0), 0), axis=1
    ) - 1
    own_cols = recv_buf.reshape(owners * cap, -1)[own_owner * cap + own_rank]
    neighbours = lax.all_gather(own_cols, "mp", axis=1, tiled=True)

    def this_half(x):
        return lax.dynamic_slice_in_dim(x, me_group * half, half, 1)

    def other_half(x):
        return lax.dynamic_slice_in_dim(x, (1 - me_group) * half, half, 1)

    query_part = jnp.dot(query_half, w_query, preferred_element_type=jnp.float32)
    query = group_sum(query_part).astype(jnp.bfloat16)
    n_here, n_there = this_half(neighbours), other_half(neighbours)
    keys = (
        jnp.dot(n_here, w_key, preferred_element_type=jnp.float32)
        + jnp.dot(n_there, wk_other, preferred_element_type=jnp.float32)
    ).astype(jnp.bfloat16)
    values = (
        jnp.dot(n_here, w_value, preferred_element_type=jnp.float32)
        + jnp.dot(n_there, wv_other, preferred_element_type=jnp.float32)
    ).astype(jnp.bfloat16)
    key_block = keys.reshape(blocks_here, RET, heads_here, HD)
    value_block = values.reshape(blocks_here, RET, heads_here, HD)
    query_block = query.reshape(blocks_here, BLOCK, heads_here, HD)
    live = (counts > me_group).astype(jnp.float32)
    scores = (
        jnp.einsum("cqhd,ckhd->chqk", query_block, key_block, preferred_element_type=jnp.float32)
        * inv_root
    )
    weights = jnp.exp(scores) * live[:, None, None, None]
    numer = jnp.einsum(
        "chqk,ckhd->cqhd",
        weights.astype(jnp.bfloat16),
        value_block,
        preferred_element_type=jnp.float32,
    )
    partial_total = jnp.sum(weights, -1)
    numer, partial_total = group_sum(numer), group_sum(partial_total)
    total = partial_total + 1.0
    attn = numer / jnp.transpose(total, (0, 2, 1))[..., None]
    attn_bf = attn.reshape(rows_here, heads_here * HD).astype(jnp.bfloat16)

    def place_half(x):
        zeros = jnp.zeros_like(x)
        return jnp.where(
            me_group == 0, jnp.concatenate([x, zeros], 1), jnp.concatenate([zeros, x], 1)
        )

    out_term = jnp.dot(attn_bf, w_out, preferred_element_type=jnp.float32)
    d_attn_part = contract(grad_half, w_out)
    d_attn = group_sum(d_attn_part).astype(jnp.bfloat16)
    d_block = d_attn.reshape(blocks_here, BLOCK, heads_here, HD)
    prob = weights / total[..., None]
    d_prob = jnp.einsum("cqhd,ckhd->chqk", d_block, value_block, preferred_element_type=jnp.float32)
    delta = jnp.sum(d_block.astype(jnp.float32) * attn, -1)
    d_score = (prob * (d_prob - jnp.transpose(delta, (0, 2, 1))[..., None])).astype(jnp.bfloat16)
    query_part = jnp.einsum(
        "chqk,ckhd->cqhd", d_score, key_block, preferred_element_type=jnp.float32
    )
    query_grad = group_sum(query_part)
    d_query = (query_grad * inv_root).astype(jnp.bfloat16).reshape(rows_here, heads_here * HD)
    d_keys = (
        jnp.einsum("chqk,cqhd->ckhd", d_score, query_block, preferred_element_type=jnp.float32)
        * inv_root
    ).astype(jnp.bfloat16)
    d_values = jnp.einsum(
        "chqk,cqhd->ckhd", prob.astype(jnp.bfloat16), d_block, preferred_element_type=jnp.float32
    ).astype(jnp.bfloat16)
    d_keys = d_keys.reshape(blocks_here * RET, heads_here * HD)
    d_values = d_values.reshape(blocks_here * RET, heads_here * HD)
    hid_term = contract(d_query, w_query)
    term_here = contract(d_keys, w_key) + contract(d_values, w_value)
    term_there = contract(d_keys, wk_other) + contract(d_values, wv_other)
    neigh_term = jnp.where(
        me_group == 0,
        jnp.concatenate([term_here, term_there], 1),
        jnp.concatenate([term_there, term_here], 1),
    )
    stacked = jnp.concatenate(
        [
            place_half(out_term.astype(jnp.bfloat16)),
            place_half(hid_term.astype(jnp.bfloat16)),
            neigh_term.astype(jnp.bfloat16),
        ],
        0,
    )
    reduced = lax.psum_scatter(stacked, "mp", scatter_dimension=1, tiled=True)
    both_cols = reduced[: 2 * rows_here]
    both_cols = (both_cols + lax.ppermute(both_cols, "group", swap)).astype(jnp.float32)
    out_cols, hid_cols = both_cols[:rows_here], both_cols[rows_here:]
    zero_rows = jnp.zeros((tail_rows, out_cols.shape[1]), jnp.float32)
    output = jnp.concatenate([zero_rows, out_cols[:keep_rows]], 0)
    grad_hidden = jnp.concatenate([zero_rows, hid_cols[:keep_rows]], 0)
    neigh_cols = reduced[2 * rows_here :].astype(jnp.float32)
    grad_neighbours = neigh_cols.reshape(blocks_here, 1, RET, neigh_cols.shape[1])
    return (output, grad_hidden, grad_neighbours)


def solution(mesh):
    return jax.shard_map(
        per_device,
        mesh=mesh,
        in_specs=(
            P("dp", "mp"),
            P("dp", "group", None),
            P("dp"),
            P(("dp", "group"), "mp"),
            P("group", "mp"),
            P("group", "mp"),
            P("group", "mp"),
            P("mp", "group"),
            P("dp", "mp"),
        ),
        out_specs=(P("dp", "mp"), P("dp", "mp"), P("dp", "group", None, "mp")),
        check_vma=False,
    )
```

```python
import math

import jax
import jax.numpy as jnp
from jax import lax
from jax.sharding import PartitionSpec as P

HD = 128
BLOCK = 64
RET = 128


def contract(left, right):
    return lax.dot_general(
        left, right, (((1,), (1,)), ((), ())), preferred_element_type=jnp.float32
    )


def per_device(
    hidden, neighbour_ids, counts, embed_table, w_query, w_key, w_value, w_out, grad_out
):
    tail_rows = BLOCK - 1
    rows_here = hidden.shape[0]
    blocks_here = rows_here // BLOCK
    heads_here = w_query.shape[1] // HD
    inv_root = 1.0 / math.sqrt(HD)
    keep_rows = rows_here - tail_rows
    half = w_query.shape[0]
    me_group = lax.axis_index("group")
    me_dp = lax.axis_index("dp")
    swap = [(0, 1), (1, 0)]

    def group_sum(x):
        return x + lax.ppermute(x, "group", swap)

    pad_rows = jnp.zeros((tail_rows, hidden.shape[1]), jnp.bfloat16)
    query_rows = jnp.concatenate([hidden[tail_rows:], pad_rows], 0)
    grad_rows = jnp.concatenate([grad_out[tail_rows:], pad_rows], 0)
    full_query = lax.all_gather(query_rows, "mp", axis=1, tiled=True)
    piece_rows = half // lax.axis_size("dp")
    kv_local = jnp.concatenate([w_key, w_value], axis=1)
    kv_piece = lax.dynamic_slice_in_dim(kv_local, me_dp * piece_rows, piece_rows, 0)
    held = lax.ppermute(kv_piece, "group", swap)[None]
    n_dp = lax.axis_size("dp")
    bit = n_dp // 2
    while bit >= 1:
        pairs = [(i, i ^ bit) for i in range(n_dp)]
        other = lax.ppermute(held, "dp", pairs)
        low = (me_dp // bit) % 2 == 0
        held = jnp.where(
            low, jnp.concatenate([held, other], 0), jnp.concatenate([other, held], 0)
        )
        bit //= 2
    n_bits = n_dp.bit_length() - 1
    held = held.reshape((2,) * n_bits + held.shape[1:])
    held = jnp.transpose(held, tuple(reversed(range(n_bits))) + (n_bits, n_bits + 1))
    kv_other = held.reshape(-1, held.shape[-1])
    cols_kv = w_key.shape[1]
    wk_other, wv_other = kv_other[:, :cols_kv], kv_other[:, cols_kv:]

    flat_ids = neighbour_ids.reshape(-1)
    block_rows = embed_table.shape[0]
    owners = lax.axis_size("dp") * lax.axis_size("group")
    cap = flat_ids.shape[0] // 4
    ids_out = jnp.broadcast_to(flat_ids.astype(jnp.float32)[None], (owners, flat_ids.shape[0]))
    every_id = lax.all_to_all(ids_out, ("dp", "group"), 0, 0, tiled=True).astype(jnp.int32)
    owner = me_dp * lax.axis_size("group") + me_group
    local_ids = every_id - owner * block_rows
    inside = (local_ids >= 0) & (local_ids < block_rows)
    rank = jnp.cumsum(inside.astype(jnp.int32), axis=1) - 1
    slot_hit = inside[:, :, None] & (rank[:, :, None] == jnp.arange(cap)[None, None, :])
    send_rows = jnp.sum(jnp.where(slot_hit, local_ids[:, :, None], 0), axis=1)
    send_buf = embed_table[send_rows.reshape(-1)].reshape(owners, cap, -1)
    recv_buf = lax.all_to_all(send_buf, ("dp", "group"), 0, 0, tiled=True)
    own_owner = flat_ids // block_rows
    same_owner = own_owner[:, None] == jnp.arange(owners)[None, :]
    own_rank = jnp.sum(
        jnp.where(same_owner, jnp.cumsum(same_owner.astype(jnp.int32), axis=0), 0), axis=1
    ) - 1
    own_cols = recv_buf.reshape(owners * cap, -1)[own_owner * cap + own_rank]
    neighbours = lax.all_gather(own_cols, "mp", axis=1, tiled=True)
    grad_rows, neighbours = lax.optimization_barrier((grad_rows, neighbours))
    full_grad = lax.all_gather(grad_rows, "mp", axis=1, tiled=True)

    def this_half(x):
        return lax.dynamic_slice_in_dim(x, me_group * half, half, 1)

    def other_half(x):
        return lax.dynamic_slice_in_dim(x, (1 - me_group) * half, half, 1)

    query_part = jnp.dot(this_half(full_query), w_query, preferred_element_type=jnp.float32)
    query = group_sum(query_part).astype(jnp.bfloat16)
    n_here, n_there = this_half(neighbours), other_half(neighbours)
    keys = (
        jnp.dot(n_here, w_key, preferred_element_type=jnp.float32)
        + jnp.dot(n_there, wk_other, preferred_element_type=jnp.float32)
    ).astype(jnp.bfloat16)
    values = (
        jnp.dot(n_here, w_value, preferred_element_type=jnp.float32)
        + jnp.dot(n_there, wv_other, preferred_element_type=jnp.float32)
    ).astype(jnp.bfloat16)
    key_block = keys.reshape(blocks_here, RET, heads_here, HD)
    value_block = values.reshape(blocks_here, RET, heads_here, HD)
    query_block = query.reshape(blocks_here, BLOCK, heads_here, HD)
    live = (counts > me_group).astype(jnp.float32)
    scores = (
        jnp.einsum("cqhd,ckhd->chqk", query_block, key_block, preferred_element_type=jnp.float32)
        * inv_root
    )
    weights = jnp.exp(scores) * live[:, None, None, None]
    numer = jnp.einsum(
        "chqk,ckhd->cqhd",
        weights.astype(jnp.bfloat16),
        value_block,
        preferred_element_type=jnp.float32,
    )
    partial_total = jnp.sum(weights, -1)
    numer, partial_total = group_sum(numer), group_sum(partial_total)
    total = partial_total + 1.0
    attn = numer / jnp.transpose(total, (0, 2, 1))[..., None]
    attn_bf = attn.reshape(rows_here, heads_here * HD).astype(jnp.bfloat16)

    def place_half(x):
        zeros = jnp.zeros_like(x)
        return jnp.where(
            me_group == 0, jnp.concatenate([x, zeros], 1), jnp.concatenate([zeros, x], 1)
        )

    out_term = jnp.dot(attn_bf, w_out, preferred_element_type=jnp.float32)
    d_attn_part = contract(this_half(full_grad), w_out)
    d_attn = group_sum(d_attn_part).astype(jnp.bfloat16)
    d_block = d_attn.reshape(blocks_here, BLOCK, heads_here, HD)
    prob = weights / total[..., None]
    d_prob = jnp.einsum("cqhd,ckhd->chqk", d_block, value_block, preferred_element_type=jnp.float32)
    delta = jnp.sum(d_block.astype(jnp.float32) * attn, -1)
    d_score = (prob * (d_prob - jnp.transpose(delta, (0, 2, 1))[..., None])).astype(jnp.bfloat16)
    query_part = jnp.einsum(
        "chqk,ckhd->cqhd", d_score, key_block, preferred_element_type=jnp.float32
    )
    query_grad = group_sum(query_part)
    d_query = (query_grad * inv_root).astype(jnp.bfloat16).reshape(rows_here, heads_here * HD)
    d_keys = (
        jnp.einsum("chqk,cqhd->ckhd", d_score, query_block, preferred_element_type=jnp.float32)
        * inv_root
    ).astype(jnp.bfloat16)
    d_values = jnp.einsum(
        "chqk,cqhd->ckhd", prob.astype(jnp.bfloat16), d_block, preferred_element_type=jnp.float32
    ).astype(jnp.bfloat16)
    d_keys = d_keys.reshape(blocks_here * RET, heads_here * HD)
    d_values = d_values.reshape(blocks_here * RET, heads_here * HD)
    hid_term = contract(d_query, w_query)
    term_here = contract(d_keys, w_key) + contract(d_values, w_value)
    term_there = contract(d_keys, wk_other) + contract(d_values, wv_other)
    neigh_term = jnp.where(
        me_group == 0,
        jnp.concatenate([term_here, term_there], 1),
        jnp.concatenate([term_there, term_here], 1),
    )
    stacked = jnp.concatenate(
        [
            place_half(out_term.astype(jnp.bfloat16)),
            place_half(hid_term.astype(jnp.bfloat16)),
            neigh_term.astype(jnp.bfloat16),
        ],
        0,
    )
    reduced = lax.psum_scatter(stacked, "mp", scatter_dimension=1, tiled=True)
    both_cols = reduced[: 2 * rows_here]
    both_cols = (both_cols + lax.ppermute(both_cols, "group", swap)).astype(jnp.float32)
    out_cols, hid_cols = both_cols[:rows_here], both_cols[rows_here:]
    zero_rows = jnp.zeros((tail_rows, out_cols.shape[1]), jnp.float32)
    output = jnp.concatenate([zero_rows, out_cols[:keep_rows]], 0)
    grad_hidden = jnp.concatenate([zero_rows, hid_cols[:keep_rows]], 0)
    neigh_cols = reduced[2 * rows_here :].astype(jnp.float32)
    grad_neighbours = neigh_cols.reshape(blocks_here, 1, RET, neigh_cols.shape[1])
    return (output, grad_hidden, grad_neighbours)


def solution(mesh):
    return jax.shard_map(
        per_device,
        mesh=mesh,
        in_specs=(
            P("dp", "mp"),
            P("dp", "group", None),
            P("dp"),
            P(("dp", "group"), "mp"),
            P("group", "mp"),
            P("group", "mp"),
            P("group", "mp"),
            P("mp", "group"),
            P("dp", "mp"),
        ),
        out_specs=(P("dp", "mp"), P("dp", "mp"), P("dp", "group", None, "mp")),
        check_vma=False,
    )
```

```python
import math

import jax
import jax.numpy as jnp
from jax import lax
from jax.sharding import PartitionSpec as P

HD = 128
BLOCK = 64
RET = 128


def contract(left, right):
    return lax.dot_general(
        left, right, (((1,), (1,)), ((), ())), preferred_element_type=jnp.float32
    )


def per_device(
    hidden, neighbour_ids, counts, embed_table, w_query, w_key, w_value, w_out, grad_out
):
    tail_rows = BLOCK - 1
    rows_here = hidden.shape[0]
    blocks_here = rows_here // BLOCK
    heads_here = w_query.shape[1] // HD
    inv_root = 1.0 / math.sqrt(HD)
    keep_rows = rows_here - tail_rows
    half = w_query.shape[0]
    me_group = lax.axis_index("group")
    me_dp = lax.axis_index("dp")
    swap = [(0, 1), (1, 0)]

    def group_sum(x):
        return x + lax.ppermute(x, "group", swap)

    pad_rows = jnp.zeros((tail_rows, hidden.shape[1]), jnp.bfloat16)
    query_rows = jnp.concatenate([hidden[tail_rows:], pad_rows], 0)
    grad_rows = jnp.concatenate([grad_out[tail_rows:], pad_rows], 0)
    full_query, full_grad = (
        lax.all_gather(query_rows, "mp", axis=1, tiled=True),
        lax.all_gather(grad_rows, "mp", axis=1, tiled=True),
    )
    piece_rows = half // lax.axis_size("dp")
    kv_local = jnp.concatenate([w_key, w_value], axis=1)
    kv_piece = lax.dynamic_slice_in_dim(kv_local, me_dp * piece_rows, piece_rows, 0)
    held = lax.ppermute(kv_piece, "group", swap)[None]
    n_dp = lax.axis_size("dp")
    bit = n_dp // 2
    while bit >= 1:
        pairs = [(i, i ^ bit) for i in range(n_dp)]
        other = lax.ppermute(held, "dp", pairs)
        low = (me_dp // bit) % 2 == 0
        held = jnp.where(
            low, jnp.concatenate([held, other], 0), jnp.concatenate([other, held], 0)
        )
        bit //= 2
    n_bits = n_dp.bit_length() - 1
    held = held.reshape((2,) * n_bits + held.shape[1:])
    held = jnp.transpose(held, tuple(reversed(range(n_bits))) + (n_bits, n_bits + 1))
    kv_other = held.reshape(-1, held.shape[-1])
    cols_kv = w_key.shape[1]
    wk_other, wv_other = kv_other[:, :cols_kv], kv_other[:, cols_kv:]

    flat_ids = neighbour_ids.reshape(-1)
    block_rows = embed_table.shape[0]
    owners = lax.axis_size("dp") * lax.axis_size("group")
    cap = flat_ids.shape[0] // 4
    ids_out = jnp.broadcast_to(flat_ids.astype(jnp.float32)[None], (owners, flat_ids.shape[0]))
    every_id = lax.all_to_all(ids_out, ("dp", "group"), 0, 0, tiled=True).astype(jnp.int32)
    owner = me_dp * lax.axis_size("group") + me_group
    local_ids = every_id - owner * block_rows
    inside = (local_ids >= 0) & (local_ids < block_rows)
    rank = jnp.cumsum(inside.astype(jnp.int32), axis=1) - 1
    slot_hit = inside[:, :, None] & (rank[:, :, None] == jnp.arange(cap)[None, None, :])
    send_rows = jnp.sum(jnp.where(slot_hit, local_ids[:, :, None], 0), axis=1)
    send_buf = embed_table[send_rows.reshape(-1)].reshape(owners, cap, -1)
    recv_buf = lax.all_to_all(send_buf, ("dp", "group"), 0, 0, tiled=True)
    own_owner = flat_ids // block_rows
    same_owner = own_owner[:, None] == jnp.arange(owners)[None, :]
    own_rank = jnp.sum(
        jnp.where(same_owner, jnp.cumsum(same_owner.astype(jnp.int32), axis=0), 0), axis=1
    ) - 1
    own_cols = recv_buf.reshape(owners * cap, -1)[own_owner * cap + own_rank]
    neighbours = lax.all_gather(own_cols, "mp", axis=1, tiled=True)

    def this_half(x):
        return lax.dynamic_slice_in_dim(x, me_group * half, half, 1)

    def other_half(x):
        return lax.dynamic_slice_in_dim(x, (1 - me_group) * half, half, 1)

    query_part = jnp.dot(this_half(full_query), w_query, preferred_element_type=jnp.float32)
    query = group_sum(query_part).astype(jnp.bfloat16)
    n_here, n_there = this_half(neighbours), other_half(neighbours)
    keys = (
        jnp.dot(n_here, w_key, preferred_element_type=jnp.float32)
        + jnp.dot(n_there, wk_other, preferred_element_type=jnp.float32)
    ).astype(jnp.bfloat16)
    values = (
        jnp.dot(n_here, w_value, preferred_element_type=jnp.float32)
        + jnp.dot(n_there, wv_other, preferred_element_type=jnp.float32)
    ).astype(jnp.bfloat16)
    key_block = keys.reshape(blocks_here, RET, heads_here, HD)
    value_block = values.reshape(blocks_here, RET, heads_here, HD)
    query_block = query.reshape(blocks_here, BLOCK, heads_here, HD)
    live = (counts > me_group).astype(jnp.float32)
    scores = (
        jnp.einsum("cqhd,ckhd->chqk", query_block, key_block, preferred_element_type=jnp.float32)
        * inv_root
    )
    weights = jnp.exp(scores) * live[:, None, None, None]
    numer = jnp.einsum(
        "chqk,ckhd->cqhd",
        weights.astype(jnp.bfloat16),
        value_block,
        preferred_element_type=jnp.float32,
    )
    partial_total = jnp.sum(weights, -1)
    numer, partial_total = group_sum(numer), group_sum(partial_total)
    total = partial_total + 1.0
    attn = numer / jnp.transpose(total, (0, 2, 1))[..., None]
    attn_bf = attn.reshape(rows_here, heads_here * HD).astype(jnp.bfloat16)

    out_term = jnp.dot(attn_bf, w_out, preferred_element_type=jnp.float32)
    d_attn_part = contract(this_half(full_grad), w_out)
    d_attn = group_sum(d_attn_part).astype(jnp.bfloat16)
    d_block = d_attn.reshape(blocks_here, BLOCK, heads_here, HD)
    prob = weights / total[..., None]
    d_prob = jnp.einsum("cqhd,ckhd->chqk", d_block, value_block, preferred_element_type=jnp.float32)
    delta = jnp.sum(d_block.astype(jnp.float32) * attn, -1)
    d_score = (prob * (d_prob - jnp.transpose(delta, (0, 2, 1))[..., None])).astype(jnp.bfloat16)
    query_part = jnp.einsum(
        "chqk,ckhd->cqhd", d_score, key_block, preferred_element_type=jnp.float32
    )
    query_grad = group_sum(query_part)
    d_query = (query_grad * inv_root).astype(jnp.bfloat16).reshape(rows_here, heads_here * HD)
    d_keys = (
        jnp.einsum("chqk,cqhd->ckhd", d_score, query_block, preferred_element_type=jnp.float32)
        * inv_root
    ).astype(jnp.bfloat16)
    d_values = jnp.einsum(
        "chqk,cqhd->ckhd", prob.astype(jnp.bfloat16), d_block, preferred_element_type=jnp.float32
    ).astype(jnp.bfloat16)
    d_keys = d_keys.reshape(blocks_here * RET, heads_here * HD)
    d_values = d_values.reshape(blocks_here * RET, heads_here * HD)
    hid_term = contract(d_query, w_query)
    term_here = contract(d_keys, w_key) + contract(d_values, w_value)
    term_there = contract(d_keys, wk_other) + contract(d_values, wv_other)
    neigh_term = jnp.where(
        me_group == 0,
        jnp.concatenate([term_here, term_there], 1),
        jnp.concatenate([term_there, term_here], 1),
    )
    packed = jnp.concatenate(
        [out_term.astype(jnp.bfloat16), hid_term.astype(jnp.bfloat16)], 1
    )
    stacked = jnp.concatenate([packed, neigh_term.astype(jnp.bfloat16)], 0)
    reduced = lax.psum_scatter(stacked, "mp", scatter_dimension=1, tiled=True)
    held_cols = reduced[:rows_here]
    n_mp = lax.axis_size("mp")
    half_mp = n_mp // 2

    def owner_of(s, gs, g_to):
        return (gs * half_mp + s % half_mp) * 2 + g_to

    pairs_a, pairs_b = [], []
    for s in range(n_mp):
        for gs in range(2):
            is_out = s < half_mp
            pairs_a.append((s * 2 + gs, owner_of(s, gs, 0 if is_out else 1)))
            pairs_b.append((s * 2 + gs, owner_of(s, gs, 1 if is_out else 0)))
    got_a = lax.ppermute(held_cols, ("mp", "group"), pairs_a)
    got_b = lax.ppermute(held_cols, ("mp", "group"), pairs_b)
    out_cols = jnp.where(me_group == 0, got_a, got_b).astype(jnp.float32)
    hid_cols = jnp.where(me_group == 0, got_b, got_a).astype(jnp.float32)
    zero_rows = jnp.zeros((tail_rows, out_cols.shape[1]), jnp.float32)
    output = jnp.concatenate([zero_rows, out_cols[:keep_rows]], 0)
    grad_hidden = jnp.concatenate([zero_rows, hid_cols[:keep_rows]], 0)
    neigh_cols = reduced[rows_here:].astype(jnp.float32)
    grad_neighbours = neigh_cols.reshape(blocks_here, 1, RET, neigh_cols.shape[1])
    return (output, grad_hidden, grad_neighbours)


def solution(mesh):
    return jax.shard_map(
        per_device,
        mesh=mesh,
        in_specs=(
            P("dp", "mp"),
            P("dp", "group", None),
            P("dp"),
            P(("dp", "group"), "mp"),
            P("group", "mp"),
            P("group", "mp"),
            P("group", "mp"),
            P("mp", "group"),
            P("dp", "mp"),
        ),
        out_specs=(P("dp", "mp"), P("dp", "mp"), P("dp", "group", None, "mp")),
        check_vma=False,
    )
```

```python
import math

import jax
import jax.numpy as jnp
from jax import lax
from jax.sharding import PartitionSpec as P

HD = 128
BLOCK = 64
RET = 128


def contract(left, right):
    return lax.dot_general(
        left, right, (((1,), (1,)), ((), ())), preferred_element_type=jnp.float32
    )


def per_device(
    hidden, neighbour_ids, counts, embed_table, w_query, w_key, w_value, w_out, grad_out
):
    tail_rows = BLOCK - 1
    rows_here = hidden.shape[0]
    blocks_here = rows_here // BLOCK
    heads_here = w_query.shape[1] // HD
    inv_root = 1.0 / math.sqrt(HD)
    keep_rows = rows_here - tail_rows
    half = w_query.shape[0]
    me_group = lax.axis_index("group")
    me_dp = lax.axis_index("dp")
    swap = [(0, 1), (1, 0)]

    def group_sum(x):
        return x + lax.ppermute(x, "group", swap)

    pad_rows = jnp.zeros((tail_rows, hidden.shape[1]), jnp.bfloat16)
    query_rows = jnp.concatenate([hidden[tail_rows:], pad_rows], 0)
    grad_rows = jnp.concatenate([grad_out[tail_rows:], pad_rows], 0)
    full_query, full_grad = (
        lax.all_gather(query_rows, "mp", axis=1, tiled=True),
        lax.all_gather(grad_rows, "mp", axis=1, tiled=True),
    )
    piece_rows = half // lax.axis_size("dp")
    kv_local = jnp.concatenate([w_key, w_value], axis=1)
    kv_piece = lax.dynamic_slice_in_dim(kv_local, me_dp * piece_rows, piece_rows, 0)
    held = lax.ppermute(kv_piece, "group", swap)[None]
    n_dp = lax.axis_size("dp")
    bit = n_dp // 2
    while bit >= 1:
        pairs = [(i, i ^ bit) for i in range(n_dp)]
        other = lax.ppermute(held, "dp", pairs)
        low = (me_dp // bit) % 2 == 0
        held = jnp.where(
            low, jnp.concatenate([held, other], 0), jnp.concatenate([other, held], 0)
        )
        bit //= 2
    n_bits = n_dp.bit_length() - 1
    held = held.reshape((2,) * n_bits + held.shape[1:])
    held = jnp.transpose(held, tuple(reversed(range(n_bits))) + (n_bits, n_bits + 1))
    kv_other = held.reshape(-1, held.shape[-1])
    cols_kv = w_key.shape[1]
    wk_other, wv_other = kv_other[:, :cols_kv], kv_other[:, cols_kv:]

    flat_ids = neighbour_ids.reshape(-1)
    block_rows = embed_table.shape[0]
    owners = lax.axis_size("dp") * lax.axis_size("group")
    cap = flat_ids.shape[0] // 4
    ids_out = jnp.broadcast_to(flat_ids.astype(jnp.float32)[None], (owners, flat_ids.shape[0]))
    every_id = lax.all_to_all(ids_out, ("dp", "group"), 0, 0, tiled=True).astype(jnp.int32)
    owner = me_dp * lax.axis_size("group") + me_group
    local_ids = every_id - owner * block_rows
    inside = (local_ids >= 0) & (local_ids < block_rows)
    rank = jnp.cumsum(inside.astype(jnp.int32), axis=1) - 1
    slot_hit = inside[:, :, None] & (rank[:, :, None] == jnp.arange(cap)[None, None, :])
    send_rows = jnp.sum(jnp.where(slot_hit, local_ids[:, :, None], 0), axis=1)
    send_buf = embed_table[send_rows.reshape(-1)].reshape(owners, cap, -1)
    recv_buf = lax.all_to_all(send_buf, ("dp", "group"), 0, 0, tiled=True)
    own_owner = flat_ids // block_rows
    same_owner = own_owner[:, None] == jnp.arange(owners)[None, :]
    own_rank = jnp.sum(
        jnp.where(same_owner, jnp.cumsum(same_owner.astype(jnp.int32), axis=0), 0), axis=1
    ) - 1
    own_cols = recv_buf.reshape(owners * cap, -1)[own_owner * cap + own_rank]
    neighbours = lax.all_gather(own_cols, "mp", axis=1, tiled=True)

    def this_half(x):
        return lax.dynamic_slice_in_dim(x, me_group * half, half, 1)

    def other_half(x):
        return lax.dynamic_slice_in_dim(x, (1 - me_group) * half, half, 1)

    query_part = jnp.dot(this_half(full_query), w_query, preferred_element_type=jnp.float32)
    query = group_sum(query_part).astype(jnp.bfloat16)
    n_here, n_there = this_half(neighbours), other_half(neighbours)
    keys = (
        jnp.dot(n_here, w_key, preferred_element_type=jnp.float32)
        + jnp.dot(n_there, wk_other, preferred_element_type=jnp.float32)
    ).astype(jnp.bfloat16)
    values = (
        jnp.dot(n_here, w_value, preferred_element_type=jnp.float32)
        + jnp.dot(n_there, wv_other, preferred_element_type=jnp.float32)
    ).astype(jnp.bfloat16)
    key_block = keys.reshape(blocks_here, RET, heads_here, HD)
    value_block = values.reshape(blocks_here, RET, heads_here, HD)
    query_block = query.reshape(blocks_here, BLOCK, heads_here, HD)
    live = (counts > me_group).astype(jnp.float32)
    scores = (
        jnp.einsum("cqhd,ckhd->chqk", query_block, key_block, preferred_element_type=jnp.float32)
        * inv_root
    )
    weights = jnp.exp(scores) * live[:, None, None, None]
    numer = jnp.einsum(
        "chqk,ckhd->cqhd",
        weights.astype(jnp.bfloat16),
        value_block,
        preferred_element_type=jnp.float32,
    )
    partial_total = jnp.sum(weights, -1)
    numer_size = numer.size
    joined = group_sum(jnp.concatenate([numer.reshape(-1), partial_total.reshape(-1)]))
    numer = joined[:numer_size].reshape(numer.shape)
    partial_total = joined[numer_size:].reshape(partial_total.shape)
    total = partial_total + 1.0
    attn = numer / jnp.transpose(total, (0, 2, 1))[..., None]
    attn_bf = attn.reshape(rows_here, heads_here * HD).astype(jnp.bfloat16)

    def place_half(x):
        zeros = jnp.zeros_like(x)
        return jnp.where(
            me_group == 0, jnp.concatenate([x, zeros], 1), jnp.concatenate([zeros, x], 1)
        )

    out_term = jnp.dot(attn_bf, w_out, preferred_element_type=jnp.float32)
    d_attn_part = contract(this_half(full_grad), w_out)
    d_attn = group_sum(d_attn_part).astype(jnp.bfloat16)
    d_block = d_attn.reshape(blocks_here, BLOCK, heads_here, HD)
    prob = weights / total[..., None]
    d_prob = jnp.einsum("cqhd,ckhd->chqk", d_block, value_block, preferred_element_type=jnp.float32)
    delta = jnp.sum(d_block.astype(jnp.float32) * attn, -1)
    d_score = (prob * (d_prob - jnp.transpose(delta, (0, 2, 1))[..., None])).astype(jnp.bfloat16)
    query_part = jnp.einsum(
        "chqk,ckhd->cqhd", d_score, key_block, preferred_element_type=jnp.float32
    )
    query_grad = group_sum(query_part)
    d_query = (query_grad * inv_root).astype(jnp.bfloat16).reshape(rows_here, heads_here * HD)
    d_keys = (
        jnp.einsum("chqk,cqhd->ckhd", d_score, query_block, preferred_element_type=jnp.float32)
        * inv_root
    ).astype(jnp.bfloat16)
    d_values = jnp.einsum(
        "chqk,cqhd->ckhd", prob.astype(jnp.bfloat16), d_block, preferred_element_type=jnp.float32
    ).astype(jnp.bfloat16)
    d_keys = d_keys.reshape(blocks_here * RET, heads_here * HD)
    d_values = d_values.reshape(blocks_here * RET, heads_here * HD)
    hid_term = contract(d_query, w_query)
    term_here = contract(d_keys, w_key) + contract(d_values, w_value)
    term_there = contract(d_keys, wk_other) + contract(d_values, wv_other)
    neigh_term = jnp.where(
        me_group == 0,
        jnp.concatenate([term_here, term_there], 1),
        jnp.concatenate([term_there, term_here], 1),
    )
    stacked = jnp.concatenate(
        [
            place_half(out_term.astype(jnp.bfloat16)),
            place_half(hid_term.astype(jnp.bfloat16)),
            neigh_term.astype(jnp.bfloat16),
        ],
        0,
    )
    reduced = lax.psum_scatter(stacked, "mp", scatter_dimension=1, tiled=True)
    both_cols = reduced[: 2 * rows_here]
    both_cols = (both_cols + lax.ppermute(both_cols, "group", swap)).astype(jnp.float32)
    out_cols, hid_cols = both_cols[:rows_here], both_cols[rows_here:]
    zero_rows = jnp.zeros((tail_rows, out_cols.shape[1]), jnp.float32)
    output = jnp.concatenate([zero_rows, out_cols[:keep_rows]], 0)
    grad_hidden = jnp.concatenate([zero_rows, hid_cols[:keep_rows]], 0)
    neigh_cols = reduced[2 * rows_here :].astype(jnp.float32)
    grad_neighbours = neigh_cols.reshape(blocks_here, 1, RET, neigh_cols.shape[1])
    return (output, grad_hidden, grad_neighbours)


def solution(mesh):
    return jax.shard_map(
        per_device,
        mesh=mesh,
        in_specs=(
            P("dp", "mp"),
            P("dp", "group", None),
            P("dp"),
            P(("dp", "group"), "mp"),
            P("group", "mp"),
            P("group", "mp"),
            P("group", "mp"),
            P("mp", "group"),
            P("dp", "mp"),
        ),
        out_specs=(P("dp", "mp"), P("dp", "mp"), P("dp", "group", None, "mp")),
        check_vma=False,
    )
```

```python
import math

import jax
import jax.numpy as jnp
from jax import lax
from jax.sharding import PartitionSpec as P

HD = 128
BLOCK = 64
RET = 128


def contract(left, right):
    return lax.dot_general(
        left, right, (((1,), (1,)), ((), ())), preferred_element_type=jnp.float32
    )


def per_device(
    hidden, neighbour_ids, counts, embed_table, w_query, w_key, w_value, w_out, grad_out
):
    tail_rows = BLOCK - 1
    rows_here = hidden.shape[0]
    blocks_here = rows_here // BLOCK
    heads_here = w_query.shape[1] // HD
    inv_root = 1.0 / math.sqrt(HD)
    keep_rows = rows_here - tail_rows
    half = w_query.shape[0]
    me_group = lax.axis_index("group")
    me_dp = lax.axis_index("dp")
    swap = [(0, 1), (1, 0)]

    def group_sum(x):
        return x + lax.ppermute(x, "group", swap)

    pad_rows = jnp.zeros((tail_rows, hidden.shape[1]), jnp.bfloat16)
    query_rows = jnp.concatenate([hidden[tail_rows:], pad_rows], 0)
    grad_rows = jnp.concatenate([grad_out[tail_rows:], pad_rows], 0)
    full_query = lax.all_gather(query_rows, "mp", axis=1, tiled=True)
    n_mp = lax.axis_size("mp")
    me_mp = lax.axis_index("mp")
    across = lax.ppermute(grad_rows, "mp", [(i, i ^ (n_mp // 2)) for i in range(n_mp)])
    held_rows = jnp.where(me_mp // (n_mp // 2) == me_group, grad_rows, across)[None]
    bit = n_mp // 4
    while bit >= 1:
        pairs = [(i, i ^ bit) for i in range(n_mp)]
        other = lax.ppermute(held_rows, "mp", pairs)
        low = (me_mp // bit) % 2 == 0
        held_rows = jnp.where(
            low,
            jnp.concatenate([held_rows, other], 0),
            jnp.concatenate([other, held_rows], 0),
        )
        bit //= 2
    m_bits = (n_mp // 2).bit_length() - 1
    held_rows = held_rows.reshape((2,) * m_bits + held_rows.shape[1:])
    held_rows = jnp.transpose(held_rows, tuple(reversed(range(m_bits))) + (m_bits, m_bits + 1))
    grad_half = jnp.transpose(
        held_rows.reshape((n_mp // 2,) + held_rows.shape[-2:]), (1, 0, 2)
    ).reshape(rows_here, half)
    piece_rows = half // lax.axis_size("dp")
    kv_local = jnp.concatenate([w_key, w_value], axis=1)
    kv_piece = lax.dynamic_slice_in_dim(kv_local, me_dp * piece_rows, piece_rows, 0)
    held = lax.ppermute(kv_piece, "group", swap)[None]
    n_dp = lax.axis_size("dp")
    bit = n_dp // 2
    while bit >= 1:
        pairs = [(i, i ^ bit) for i in range(n_dp)]
        other = lax.ppermute(held, "dp", pairs)
        low = (me_dp // bit) % 2 == 0
        held = jnp.where(
            low, jnp.concatenate([held, other], 0), jnp.concatenate([other, held], 0)
        )
        bit //= 2
    n_bits = n_dp.bit_length() - 1
    held = held.reshape((2,) * n_bits + held.shape[1:])
    held = jnp.transpose(held, tuple(reversed(range(n_bits))) + (n_bits, n_bits + 1))
    kv_other = held.reshape(-1, held.shape[-1])
    cols_kv = w_key.shape[1]
    wk_other, wv_other = kv_other[:, :cols_kv], kv_other[:, cols_kv:]

    flat_ids = neighbour_ids.reshape(-1)
    block_rows = embed_table.shape[0]
    owners = lax.axis_size("dp") * lax.axis_size("group")
    cap = flat_ids.shape[0] // 4
    ids_out = jnp.broadcast_to(flat_ids.astype(jnp.float32)[None], (owners, flat_ids.shape[0]))
    every_id = lax.all_to_all(ids_out, ("dp", "group"), 0, 0, tiled=True).astype(jnp.int32)
    owner = me_dp * lax.axis_size("group") + me_group
    local_ids = every_id - owner * block_rows
    inside = (local_ids >= 0) & (local_ids < block_rows)
    rank = jnp.cumsum(inside.astype(jnp.int32), axis=1) - 1
    slot_hit = inside[:, :, None] & (rank[:, :, None] == jnp.arange(cap)[None, None, :])
    send_rows = jnp.sum(jnp.where(slot_hit, local_ids[:, :, None], 0), axis=1)
    send_buf = embed_table[send_rows.reshape(-1)].reshape(owners, cap, -1)
    recv_buf = lax.all_to_all(send_buf, ("dp", "group"), 0, 0, tiled=True)
    own_owner = flat_ids // block_rows
    same_owner = own_owner[:, None] == jnp.arange(owners)[None, :]
    own_rank = jnp.sum(
        jnp.where(same_owner, jnp.cumsum(same_owner.astype(jnp.int32), axis=0), 0), axis=1
    ) - 1
    own_cols = recv_buf.reshape(owners * cap, -1)[own_owner * cap + own_rank]
    neighbours = lax.all_gather(own_cols, "mp", axis=1, tiled=True)

    def this_half(x):
        return lax.dynamic_slice_in_dim(x, me_group * half, half, 1)

    def other_half(x):
        return lax.dynamic_slice_in_dim(x, (1 - me_group) * half, half, 1)

    query_part = jnp.dot(this_half(full_query), w_query, preferred_element_type=jnp.float32)
    query = group_sum(query_part).astype(jnp.bfloat16)
    n_here, n_there = this_half(neighbours), other_half(neighbours)
    keys = (
        jnp.dot(n_here, w_key, preferred_element_type=jnp.float32)
        + jnp.dot(n_there, wk_other, preferred_element_type=jnp.float32)
    ).astype(jnp.bfloat16)
    values = (
        jnp.dot(n_here, w_value, preferred_element_type=jnp.float32)
        + jnp.dot(n_there, wv_other, preferred_element_type=jnp.float32)
    ).astype(jnp.bfloat16)
    key_block = keys.reshape(blocks_here, RET, heads_here, HD)
    value_block = values.reshape(blocks_here, RET, heads_here, HD)
    query_block = query.reshape(blocks_here, BLOCK, heads_here, HD)
    live = (counts > me_group).astype(jnp.float32)
    scores = (
        jnp.einsum("cqhd,ckhd->chqk", query_block, key_block, preferred_element_type=jnp.float32)
        * inv_root
    )
    weights = jnp.exp(scores) * live[:, None, None, None]
    numer = jnp.einsum(
        "chqk,ckhd->cqhd",
        weights.astype(jnp.bfloat16),
        value_block,
        preferred_element_type=jnp.float32,
    )
    partial_total = jnp.sum(weights, -1)
    numer, partial_total = group_sum(numer), group_sum(partial_total)
    total = partial_total + 1.0
    attn = numer / jnp.transpose(total, (0, 2, 1))[..., None]
    attn_bf = attn.reshape(rows_here, heads_here * HD).astype(jnp.bfloat16)

    def place_half(x):
        zeros = jnp.zeros_like(x)
        return jnp.where(
            me_group == 0, jnp.concatenate([x, zeros], 1), jnp.concatenate([zeros, x], 1)
        )

    out_term = jnp.dot(attn_bf, w_out, preferred_element_type=jnp.float32)
    d_attn_part = contract(grad_half, w_out)
    d_attn = group_sum(d_attn_part).astype(jnp.bfloat16)
    d_block = d_attn.reshape(blocks_here, BLOCK, heads_here, HD)
    prob = weights / total[..., None]
    d_prob = jnp.einsum("cqhd,ckhd->chqk", d_block, value_block, preferred_element_type=jnp.float32)
    delta = jnp.sum(d_block.astype(jnp.float32) * attn, -1)
    d_score = (prob * (d_prob - jnp.transpose(delta, (0, 2, 1))[..., None])).astype(jnp.bfloat16)
    query_part = jnp.einsum(
        "chqk,ckhd->cqhd", d_score, key_block, preferred_element_type=jnp.float32
    )
    query_grad = group_sum(query_part)
    d_query = (query_grad * inv_root).astype(jnp.bfloat16).reshape(rows_here, heads_here * HD)
    d_keys = (
        jnp.einsum("chqk,cqhd->ckhd", d_score, query_block, preferred_element_type=jnp.float32)
        * inv_root
    ).astype(jnp.bfloat16)
    d_values = jnp.einsum(
        "chqk,cqhd->ckhd", prob.astype(jnp.bfloat16), d_block, preferred_element_type=jnp.float32
    ).astype(jnp.bfloat16)
    d_keys = d_keys.reshape(blocks_here * RET, heads_here * HD)
    d_values = d_values.reshape(blocks_here * RET, heads_here * HD)
    hid_term = contract(d_query, w_query)
    term_here = contract(d_keys, w_key) + contract(d_values, w_value)
    term_there = contract(d_keys, wk_other) + contract(d_values, wv_other)
    neigh_term = jnp.where(
        me_group == 0,
        jnp.concatenate([term_here, term_there], 1),
        jnp.concatenate([term_there, term_here], 1),
    )
    stacked = jnp.concatenate(
        [
            place_half(out_term.astype(jnp.bfloat16)),
            place_half(hid_term.astype(jnp.bfloat16)),
            neigh_term.astype(jnp.bfloat16),
        ],
        0,
    )
    reduced = lax.psum_scatter(stacked, "mp", scatter_dimension=1, tiled=True)
    both_cols = reduced[: 2 * rows_here]
    both_cols = (both_cols + lax.ppermute(both_cols, "group", swap)).astype(jnp.float32)
    out_cols, hid_cols = both_cols[:rows_here], both_cols[rows_here:]
    zero_rows = jnp.zeros((tail_rows, out_cols.shape[1]), jnp.float32)
    output = jnp.concatenate([zero_rows, out_cols[:keep_rows]], 0)
    grad_hidden = jnp.concatenate([zero_rows, hid_cols[:keep_rows]], 0)
    neigh_cols = reduced[2 * rows_here :].astype(jnp.float32)
    grad_neighbours = neigh_cols.reshape(blocks_here, 1, RET, neigh_cols.shape[1])
    return (output, grad_hidden, grad_neighbours)


def solution(mesh):
    return jax.shard_map(
        per_device,
        mesh=mesh,
        in_specs=(
            P("dp", "mp"),
            P("dp", "group", None),
            P("dp"),
            P(("dp", "group"), "mp"),
            P("group", "mp"),
            P("group", "mp"),
            P("group", "mp"),
            P("mp", "group"),
            P("dp", "mp"),
        ),
        out_specs=(P("dp", "mp"), P("dp", "mp"), P("dp", "group", None, "mp")),
        check_vma=False,
    )
```

```python
import math

import jax
import jax.numpy as jnp
from jax import lax
from jax.sharding import PartitionSpec as P

HD = 128
BLOCK = 64
RET = 128


def contract(left, right):
    return lax.dot_general(
        left, right, (((1,), (1,)), ((), ())), preferred_element_type=jnp.float32
    )


def per_device(
    hidden, neighbour_ids, counts, embed_table, w_query, w_key, w_value, w_out, grad_out
):
    tail_rows = BLOCK - 1
    rows_here = hidden.shape[0]
    blocks_here = rows_here // BLOCK
    heads_here = w_query.shape[1] // HD
    inv_root = 1.0 / math.sqrt(HD)
    keep_rows = rows_here - tail_rows
    half = w_query.shape[0]
    me_group = lax.axis_index("group")
    me_dp = lax.axis_index("dp")
    swap = [(0, 1), (1, 0)]

    def group_sum(x):
        return x + lax.ppermute(x, "group", swap)

    pad_rows = jnp.zeros((tail_rows, hidden.shape[1]), jnp.bfloat16)
    query_rows = jnp.concatenate([hidden[tail_rows:], pad_rows], 0)
    grad_rows = jnp.concatenate([grad_out[tail_rows:], pad_rows], 0)
    full_rows = lax.all_gather(jnp.stack([query_rows, grad_rows]), "mp", axis=2, tiled=True)
    full_query, full_grad = full_rows[0], full_rows[1]
    piece_rows = half // lax.axis_size("dp")
    kv_local = jnp.concatenate([w_key, w_value], axis=1)
    kv_piece = lax.dynamic_slice_in_dim(kv_local, me_dp * piece_rows, piece_rows, 0)
    held = lax.ppermute(kv_piece, "group", swap)[None]
    n_dp = lax.axis_size("dp")
    bit = n_dp // 2
    while bit >= 1:
        pairs = [(i, i ^ bit) for i in range(n_dp)]
        other = lax.ppermute(held, "dp", pairs)
        low = (me_dp // bit) % 2 == 0
        held = jnp.where(
            low, jnp.concatenate([held, other], 0), jnp.concatenate([other, held], 0)
        )
        bit //= 2
    n_bits = n_dp.bit_length() - 1
    held = held.reshape((2,) * n_bits + held.shape[1:])
    held = jnp.transpose(held, tuple(reversed(range(n_bits))) + (n_bits, n_bits + 1))
    kv_other = held.reshape(-1, held.shape[-1])
    cols_kv = w_key.shape[1]
    wk_other, wv_other = kv_other[:, :cols_kv], kv_other[:, cols_kv:]

    flat_ids = neighbour_ids.reshape(-1)
    block_rows = embed_table.shape[0]
    owners = lax.axis_size("dp") * lax.axis_size("group")
    cap = flat_ids.shape[0] // 4
    ids_out = jnp.broadcast_to(flat_ids.astype(jnp.float32)[None], (owners, flat_ids.shape[0]))
    every_id = lax.all_to_all(ids_out, ("dp", "group"), 0, 0, tiled=True).astype(jnp.int32)
    owner = me_dp * lax.axis_size("group") + me_group
    local_ids = every_id - owner * block_rows
    inside = (local_ids >= 0) & (local_ids < block_rows)
    rank = jnp.cumsum(inside.astype(jnp.int32), axis=1) - 1
    slot_hit = inside[:, :, None] & (rank[:, :, None] == jnp.arange(cap)[None, None, :])
    send_rows = jnp.sum(jnp.where(slot_hit, local_ids[:, :, None], 0), axis=1)
    send_buf = embed_table[send_rows.reshape(-1)].reshape(owners, cap, -1)
    recv_buf = lax.all_to_all(send_buf, ("dp", "group"), 0, 0, tiled=True)
    own_owner = flat_ids // block_rows
    same_owner = own_owner[:, None] == jnp.arange(owners)[None, :]
    own_rank = jnp.sum(
        jnp.where(same_owner, jnp.cumsum(same_owner.astype(jnp.int32), axis=0), 0), axis=1
    ) - 1
    own_cols = recv_buf.reshape(owners * cap, -1)[own_owner * cap + own_rank]
    neighbours = lax.all_gather(own_cols, "mp", axis=1, tiled=True)

    def this_half(x):
        return lax.dynamic_slice_in_dim(x, me_group * half, half, 1)

    def other_half(x):
        return lax.dynamic_slice_in_dim(x, (1 - me_group) * half, half, 1)

    query_part = jnp.dot(this_half(full_query), w_query, preferred_element_type=jnp.float32)
    query = group_sum(query_part).astype(jnp.bfloat16)
    n_here, n_there = this_half(neighbours), other_half(neighbours)
    keys = (
        jnp.dot(n_here, w_key, preferred_element_type=jnp.float32)
        + jnp.dot(n_there, wk_other, preferred_element_type=jnp.float32)
    ).astype(jnp.bfloat16)
    values = (
        jnp.dot(n_here, w_value, preferred_element_type=jnp.float32)
        + jnp.dot(n_there, wv_other, preferred_element_type=jnp.float32)
    ).astype(jnp.bfloat16)
    key_block = keys.reshape(blocks_here, RET, heads_here, HD)
    value_block = values.reshape(blocks_here, RET, heads_here, HD)
    query_block = query.reshape(blocks_here, BLOCK, heads_here, HD)
    live = (counts > me_group).astype(jnp.float32)
    scores = (
        jnp.einsum("cqhd,ckhd->chqk", query_block, key_block, preferred_element_type=jnp.float32)
        * inv_root
    )
    weights = jnp.exp(scores) * live[:, None, None, None]
    numer = jnp.einsum(
        "chqk,ckhd->cqhd",
        weights.astype(jnp.bfloat16),
        value_block,
        preferred_element_type=jnp.float32,
    )
    partial_total = jnp.sum(weights, -1)
    numer, partial_total = group_sum(numer), group_sum(partial_total)
    total = partial_total + 1.0
    attn = numer / jnp.transpose(total, (0, 2, 1))[..., None]
    attn_bf = attn.reshape(rows_here, heads_here * HD).astype(jnp.bfloat16)

    def place_half(x):
        zeros = jnp.zeros_like(x)
        return jnp.where(
            me_group == 0, jnp.concatenate([x, zeros], 1), jnp.concatenate([zeros, x], 1)
        )

    out_term = jnp.dot(attn_bf, w_out, preferred_element_type=jnp.float32)
    d_attn_part = contract(this_half(full_grad), w_out)
    d_attn = group_sum(d_attn_part).astype(jnp.bfloat16)
    d_block = d_attn.reshape(blocks_here, BLOCK, heads_here, HD)
    prob = weights / total[..., None]
    d_prob = jnp.einsum("cqhd,ckhd->chqk", d_block, value_block, preferred_element_type=jnp.float32)
    delta = jnp.sum(d_block.astype(jnp.float32) * attn, -1)
    d_score = (prob * (d_prob - jnp.transpose(delta, (0, 2, 1))[..., None])).astype(jnp.bfloat16)
    query_part = jnp.einsum(
        "chqk,ckhd->cqhd", d_score, key_block, preferred_element_type=jnp.float32
    )
    query_grad = group_sum(query_part)
    d_query = (query_grad * inv_root).astype(jnp.bfloat16).reshape(rows_here, heads_here * HD)
    d_keys = (
        jnp.einsum("chqk,cqhd->ckhd", d_score, query_block, preferred_element_type=jnp.float32)
        * inv_root
    ).astype(jnp.bfloat16)
    d_values = jnp.einsum(
        "chqk,cqhd->ckhd", prob.astype(jnp.bfloat16), d_block, preferred_element_type=jnp.float32
    ).astype(jnp.bfloat16)
    d_keys = d_keys.reshape(blocks_here * RET, heads_here * HD)
    d_values = d_values.reshape(blocks_here * RET, heads_here * HD)
    hid_term = contract(d_query, w_query)
    term_here = contract(d_keys, w_key) + contract(d_values, w_value)
    term_there = contract(d_keys, wk_other) + contract(d_values, wv_other)
    neigh_term = jnp.where(
        me_group == 0,
        jnp.concatenate([term_here, term_there], 1),
        jnp.concatenate([term_there, term_here], 1),
    )
    stacked = jnp.concatenate(
        [
            place_half(out_term.astype(jnp.bfloat16)),
            place_half(hid_term.astype(jnp.bfloat16)),
            neigh_term.astype(jnp.bfloat16),
        ],
        0,
    )
    reduced = lax.psum_scatter(stacked, "mp", scatter_dimension=1, tiled=True)
    both_cols = reduced[: 2 * rows_here]
    both_cols = (both_cols + lax.ppermute(both_cols, "group", swap)).astype(jnp.float32)
    out_cols, hid_cols = both_cols[:rows_here], both_cols[rows_here:]
    zero_rows = jnp.zeros((tail_rows, out_cols.shape[1]), jnp.float32)
    output = jnp.concatenate([zero_rows, out_cols[:keep_rows]], 0)
    grad_hidden = jnp.concatenate([zero_rows, hid_cols[:keep_rows]], 0)
    neigh_cols = reduced[2 * rows_here :].astype(jnp.float32)
    grad_neighbours = neigh_cols.reshape(blocks_here, 1, RET, neigh_cols.shape[1])
    return (output, grad_hidden, grad_neighbours)


def solution(mesh):
    return jax.shard_map(
        per_device,
        mesh=mesh,
        in_specs=(
            P("dp", "mp"),
            P("dp", "group", None),
            P("dp"),
            P(("dp", "group"), "mp"),
            P("group", "mp"),
            P("group", "mp"),
            P("group", "mp"),
            P("mp", "group"),
            P("dp", "mp"),
        ),
        out_specs=(P("dp", "mp"), P("dp", "mp"), P("dp", "group", None, "mp")),
        check_vma=False,
    )
```
